256 devices in a mesh: row: 8 (over y, z_hi), col: 32 (over z_lo, x, core).
Axes of the slice: x: 4, y: 4, z: 8 (z_hi: 2, z_lo: 4; z = z_hi * 4 + z_lo), core: 2. Of those that a mesh axis runs over, the one named last changes fastest.
Arguments:
- p_values: bfloat16 [8192, 8192], P('row', 'col'), may hold values from -0.164701961 to 0.164701961, as said below
- occupancy: int32 [64, 64], replicated, may hold values from 0 to 1, as said below
- square_pattern: int32 [64, 64], replicated, may hold values 0 or 1
- cube_pattern: int32 [64, 64], replicated, may hold values 0 or 1
- block_order: int32 [64], replicated, may hold values from 0 to 63, each once
Outputs:
- purified: float32 [8192, 8192], P('row', 'col')
The draws below stay inside these ranges and needn't reach their ends.
Inputs may be any that keep to these rules, and one draw needn't show every extreme that they name: p_values is symmetric. occupancy is 1 on the diagonal and on the 8 diagonals above it, 0 below the diagonal and beyond 3 * (8) diagonals above it, and 0 or 1 in between.
All inputs are finite; a program needn't handle non-finite values.
Results may differ from the reference program's by a relative error of at most 0.0016.
Values may be sent and summed in bfloat16 or wider, within the bound.
A program may use at most 128 MiB of HBM per device.

```python
import math
import jax
import jax.numpy as jnp

N = 8192
NB = 64


def draw_p_values(key, part):
    key_values = jax.random.fold_in(jax.random.fold_in(key, 11), 0)
    spread_scale = 1.0 / (0.45 * N) ** 0.5
    raw_values = jnp.clip(jax.random.normal(key_values, (N, N), jnp.float32), -4.0, 4.0)
    mirrored_values = (raw_values + raw_values.T) / math.sqrt(2.0)
    return (mirrored_values * spread_scale).astype(jnp.bfloat16)


def draw_occupancy(key, part):
    band_width = NB // 8
    row_index = jnp.arange(NB, dtype=jnp.int32)[:, None]
    col_index = jnp.arange(NB, dtype=jnp.int32)[None, :]
    offset_diag = col_index - row_index
    chosen = jax.random.randint(jax.random.fold_in(key, 23), (NB, NB), 0, 10) < 3
    inside = (offset_diag >= 0) & ((offset_diag <= band_width) | (offset_diag <= 3 * band_width) & chosen)
    return inside.astype(jnp.int32)


def place_ends(values, stream_key, low, high):
    longest = values.shape.index(max(values.shape))
    spots = []
    for shift in (0, 1):
        where = [jax.random.randint(jax.random.fold_in(stream_key, axis), (), 0, length) for axis, length in enumerate(values.shape)]
        where[longest] = (where[longest] + shift) % values.shape[longest]
        spots.append(tuple(where))
    return values.at[spots[0]].set(low).at[spots[1]].set(high)


def setup_inputs(seed: int = 0) -> dict:
    arg_keys = jax.random.split(jax.random.key(seed), 6)
    p_values = draw_p_values(jax.random.fold_in(arg_keys[5], 71), 0)
    occupancy = draw_occupancy(jax.random.fold_in(arg_keys[5], 71), 0)
    square_pattern = place_ends((jax.random.randint(arg_keys[2], (NB, NB), 0, 4) < 3).astype(jnp.int32), jax.random.fold_in(arg_keys[2], 1), 0, 1)
    cube_pattern = place_ends((jax.random.randint(arg_keys[3], (NB, NB), 0, 4) < 3).astype(jnp.int32), jax.random.fold_in(arg_keys[3], 1), 0, 1)
    block_order = jax.random.permutation(arg_keys[4], NB).astype(jnp.int32)
    return {"p_values": p_values, "occupancy": occupancy, "square_pattern": square_pattern, "cube_pattern": cube_pattern, "block_order": block_order}


def mirrored(upper_part):
    return jnp.triu(upper_part) + jnp.triu(upper_part, 1).T


def expand(upper_part, block_order, block_width):
    placed = mirrored(upper_part)[block_order][:, block_order]
    return jnp.repeat(jnp.repeat(placed, block_width, axis=0), block_width, axis=1) > 0


def reference(p_values, occupancy, square_pattern, cube_pattern, block_order):
    block_width = p_values.shape[0] // occupancy.shape[0]
    p_masked = jnp.where(expand(occupancy, block_order, block_width), p_values, jnp.zeros_like(p_values))
    squared = jnp.dot(p_masked, p_masked, preferred_element_type=jnp.float32)
    squared = jnp.where(expand(square_pattern, block_order, block_width), squared, jnp.zeros_like(squared))
    square_half = squared.astype(jnp.bfloat16)
    cubed = jnp.dot(p_masked, square_half, preferred_element_type=jnp.float32)
    cubed = jnp.where(expand(cube_pattern, block_order, block_width), cubed, jnp.zeros_like(cubed))
    return 3.0 * squared - 2.0 * cubed
```

```python
import functools
import jax
import jax.numpy as jnp
from jax import lax
from jax.experimental import pallas as pl
from jax.experimental.pallas import tpu as pltpu
from jax.sharding import Mesh
from jax.sharding import PartitionSpec as P

AXES = ("y", "zh", "zl", "x", "core")
CHUNKS = 4
ORDER = (
    ("X", 1, 0, 0), ("X", -1, 3, 0), ("Z", 0, 0), ("Y", 1, 0, 0, 3), ("Y", -1, 0, 0, 1), ("X", -1, 1, 0), ("Z", 1, 0),
    ("X", -1, 2, 0), ("X", 1, 1, 0), ("X", -1, 0, 0), ("Y", 1, 0, 0, 2), ("Z", 0, 1), ("Y", 1, 0, 0, 0), ("X", 1, 0, 1),
    ("X", 1, 2, 0), ("YF", 1, 0, 0, 2), ("Z", 2, 0), ("Y", -1, 0, 0, 0), ("Z", 0, 2), ("Y", 1, 0, 0, 1), ("XF", 1, 0, 1),
    ("X", 1, 0, 2), ("X", -1, 0, 1), ("X", -1, 0, 2), ("Z", 0, 3), ("YF", 1, 0, 0, 0), ("Y", -1, 0, 0, 3), ("X", 1, 3, 0),
    ("Z", 1, 1), ("X", -1, 0, 3), ("XF", 1, 0, 0), ("Z", 3, 0), ("XF", -1, 0, 2), ("Y", -1, 0, 0, 2), ("X", 1, 0, 3),
    ("Z", 1, 2), ("Z", 2, 1), ("YF", -1, 0, 0, 3), ("YF", -1, 0, 0, 1), ("XF", 1, 1, 0), ("XF", -1, 0, 3), ("SIB", 0, 0),
    ("Z", 1, 3), ("X", 1, 1, 1), ("X", -1, 1, 3), ("Y", 1, 0, 1, 0), ("X", -1, 1, 2), ("SIB", 1, 0), ("X", -1, 1, 1),
    ("X", 1, 1, 3), ("Z", 2, 2), ("SIB", 0, 2), ("Z", 3, 1), ("SIB", 0, -1), ("Y", -1, 0, 1, 0), ("SIB", 0, 1),
    ("X", 1, 1, 2), ("XF", -1, 1, 3), ("YF", 1, 0, 1, 0), ("Y", 1, 0, 1, 1), ("Z", 2, 3), ("Y", -1, 0, 1, 1), ("Z", 3, 2),
    ("SQ", 0, 0), ("XF", 1, 1, 1), ("XF", -1, 1, 2), ("YF", -1, 0, 1, 1), ("Z", 3, 3), ("SIB", 2, 0), ("Y", -1, 0, 1, 2),
    ("SIB", 1, -1), ("X", -1, 2, 3), ("X", 1, 2, 1), ("X", 1, 2, 3), ("Y", 1, 0, 1, 2), ("SIB", 1, 1), ("Y", -1, 0, 1, 3),
    ("SIB", 1, 2), ("Y", 1, 0, 1, 3), ("X", -1, 2, 2), ("X", -1, 2, 1), ("YF", 1, 0, 1, 2), ("SQ", 1, 0), ("X", 1, 2, 2),
    ("XF", 1, 2, 0), ("YF", -1, 0, 1, 3), ("XF", 1, 2, 1), ("XF", -1, 2, 2), ("XF", -1, 2, 3), ("SQ", 0, 1), ("ES", 0),
    ("Y", 1, 1, 0, 0), ("SQ", 1, 1), ("ES", 1), ("SIB", 2, -1), ("X", 1, 3, 3), ("SIB", 2, 1), ("Y", -1, 1, 0, 1),
    ("X", 1, 3, 1), ("SIB", 3, 0), ("X", -1, 3, 3), ("SIB", 2, 2), ("X", -1, 3, 1), ("Y", 1, 1, 0, 1), ("X", -1, 3, 2),
    ("YF", 1, 1, 0, 0), ("YF", -1, 1, 0, 1), ("X", 1, 3, 2), ("SQ", 2, 0), ("Y", 1, 1, 1, 0), ("SQ", 2, 1), ("ES", 2),
    ("Y", -1, 1, 0, 0), ("XF", -1, 3, 3), ("SIB", 3, -1), ("XF", 1, 3, 0), ("Y", -1, 1, 1, 1), ("Y", 1, 1, 0, 2),
    ("Y", -1, 1, 1, 0), ("XF", 1, 3, 1), ("XF", -1, 3, 2), ("YF", 1, 1, 1, 0), ("Y", 1, 1, 1, 2), ("Y", 1, 1, 1, 1),
    ("Y", -1, 1, 0, 2), ("SIB", 3, 1), ("SIB", 3, 2), ("YF", -1, 1, 1, 1), ("SQ", 3, 0), ("SQ", 3, 1), ("Y", -1, 1, 0, 3),
    ("CU", 0, 2, 0), ("Y", 1, 1, 0, 3), ("YF", 1, 1, 1, 2), ("YF", 1, 1, 0, 2), ("ES", 3), ("CU", 1, 2, 0), ("CU", 0, 0, 0),
    ("CU", 1, -1, 1), ("CU", 1, 0, 1), ("CU", 1, -1, 0), ("CU", 1, 2, 1), ("CU", 0, 2, 1), ("Y", -1, 1, 1, 2),
    ("CU", 0, 1, 2), ("CU", 0, 0, 1), ("YF", -1, 1, 0, 3), ("CU", 1, 1, 1), ("CU", 0, -1, 0), ("CU", 0, -1, 1),
    ("CU", 1, 0, 2), ("Y", 1, 1, 1, 3), ("CU", 0, 1, 0), ("CU", 0, 0, 2), ("Y", -1, 1, 1, 3), ("CU", 0, 0, 3),
    ("YF", -1, 1, 1, 3), ("CU", 1, 1, 0), ("CU", 1, -1, 2), ("CU", 0, 1, 3), ("CU", 0, -1, 2), ("CU", 1, 0, 0),
    ("CU", 1, 1, 2), ("CU", 0, -1, 3), ("CU", 0, 1, 1), ("CU", 0, 2, 2), ("CU", 1, 2, 2), ("CU", 1, -1, 3), ("CU", 1, 1, 3),
    ("CU", 1, 0, 3), ("CU", 0, 2, 3), ("CU", 1, 2, 3),
)


def mod4(v):
    return lax.rem(v + 8, 4)


class Step:
    def __init__(self, refs):
        (self.order, self.occupancy, self.square_pattern, self.cube_pattern, self.p, self.out, self.panel, self.p_cols,
         self.s_cols, self.square, self.cube, self.z_send, self.z_recv, self.e_send, self.x_send, self.x_recv, self.y_send,
         self.y_recv, self.sib_send, self.sib_recv) = refs
        self.y, self.zh, self.zl, self.x, self.core = (lax.axis_index(name) for name in AXES)
        self.z = self.zh * 4 + self.zl
        self.step = self.p.shape[0] // CHUNKS
        self.waited = set()
        self.sent = []
        pair = lax.rem(self.zl, 2)
        half = self.zl // 2
        self.places = (self.zl, self.zl + 1 - 2 * pair, 2 - half, 3 - 3 * half)

    def at_x(self, d):
        return {"x": mod4(self.x + d)}

    def at_y(self, d):
        return {"y": mod4(self.y + d)}

    def at_z(self, d):
        z = lax.rem(self.z + d + 8, 8)
        return {"zh": z // 4, "zl": lax.rem(z, 4)}

    def other_core(self):
        return {"core": 1 - self.core}

    def rows(self, j):
        return pl.ds(j * self.step, self.step)

    def panel_at(self, x, zl, j):
        return self.panel.at[self.core, x * 4 + zl, self.rows(j)]

    def group(self, h, d):
        return 2 * mod4(self.y + d) + (self.zh if h == 0 else 1 - self.zh)

    def cols_at(self, phase, h, d, j):
        return (self.p_cols if phase == 0 else self.s_cols).at[self.group(h, d), self.rows(j)]

    def send(self, src, dst, send_sem, recv_sem, device, guard=None):
        copy = pltpu.make_async_remote_copy(
            src_ref=src, dst_ref=dst, send_sem=send_sem, recv_sem=recv_sem, device_id=device,
            device_id_type=pl.DeviceIdType.MESH)
        if guard is None:
            copy.start()
        else:
            pl.when(guard)(copy.start)
        self.sent.append((copy, guard))

    def arrived(self, key, dst, recv_sem, guard=None):
        if key in self.waited:
            return
        self.waited.add(key)
        copy = pltpu.make_async_remote_copy(
            src_ref=dst, dst_ref=dst, send_sem=recv_sem, recv_sem=recv_sem, device_id=self.other_core(),
            device_id_type=pl.DeviceIdType.MESH)
        if guard is None:
            copy.wait_recv()
        else:
            pl.when(guard)(copy.wait_recv)

    def x_arrived(self, g, j, o):
        self.arrived(("x", g, j, o), self.panel_at(mod4(self.x + g), self.places[o], j), self.x_recv.at[g % 4, j, o])

    def y_arrived(self, phase, h, d, j):
        self.arrived(("y", phase, h, d, j), self.cols_at(phase, h, d, j), self.y_recv.at[phase, h, d % 4, j])

    def Z(self, j, d):
        zl = self.zl
        if d > 0:
            self.arrived(("z", j, d, 0), self.panel_at(self.x, lax.max(zl - d, 0), j), self.z_recv.at[0, j, d], zl >= d)
            self.arrived(("z", j, d, 1), self.panel_at(self.x, lax.min(zl + d, 3), j), self.z_recv.at[1, j, d], zl <= 3 - d)
        if d < 3:
            low = self.panel_at(self.x, lax.max(zl - d, 0), j)
            high = self.panel_at(self.x, lax.min(zl + d, 3), j)
            up, down = (zl >= d) & (zl < 3), (zl <= 3 - d) & (zl > 0)
            self.send(low, low, self.z_send.at[0, j, d], self.z_recv.at[0, j, d + 1], self.at_z(1), up)
            self.send(high, high, self.z_send.at[1, j, d], self.z_recv.at[1, j, d + 1], self.at_z(-1), down)
        if d >= 2:
            far = 4 - d
            mine = self.p_cols.at[2 * self.y + self.zh, self.rows(j)]
            self.send(self.panel_at(self.x, 3 - d, j), mine, self.e_send.at[0, 0, j, far - 1], self.y_recv.at[0, 1, 0, j],
                      self.at_z(far), zl == 3)
            self.send(self.panel_at(self.x, d, j), mine, self.e_send.at[0, 1, j, far - 1], self.y_recv.at[0, 1, 0, j],
                      self.at_z(-far), zl == 0)

    def X(self, sign, j, o):
        tile = self.panel_at(self.x, self.places[o], j)
        self.send(tile, tile, self.x_send.at[(1 - sign) // 2, 0, j, o], self.x_recv.at[-sign % 4, j, o], self.at_x(sign))

    def XF(self, sign, j, o):
        self.x_arrived(-sign, j, o)
        tile = self.panel_at(mod4(self.x - sign), self.places[o], j)
        self.send(tile, tile, self.x_send.at[(1 - sign) // 2, 1, j, o], self.x_recv.at[2, j, o], self.at_x(sign))

    def Y(self, sign, phase, h, j):
        if h == 1:
            self.y_arrived(phase, 1, 0, j)
        tile = self.cols_at(phase, h, 0, j)
        self.send(tile, tile, self.y_send.at[phase, (1 - sign) // 2, h, 0, j], self.y_recv.at[phase, h, -sign % 4, j],
                  self.at_y(sign))

    def YF(self, sign, phase, h, j):
        self.y_arrived(phase, h, -sign, j)
        tile = self.cols_at(phase, h, -sign, j)
        self.send(tile, tile, self.y_send.at[phase, (1 - sign) // 2, h, 1, j], self.y_recv.at[phase, h, 2, j], self.at_y(sign))

    def ES(self, j):
        tile = self.cols_at(1, 0, 0, j)
        self.send(tile, tile, self.e_send.at[1, 0, j, 0], self.y_recv.at[1, 1, 0, j], self.at_z(4))

    def SIB(self, j, g):
        if g != 0:
            for o in range(4):
                self.x_arrived(g, j, o)
        tiles = self.panel.at[self.core, pl.ds(mod4(self.x + g) * 4, 4), self.rows(j)]
        self.send(tiles, tiles, self.sib_send.at[j, g % 4], self.sib_recv.at[j, g % 4], self.other_core())

    def sibling_arrived(self, j):
        for g in (0, -1, 1, 2):
            tiles = self.panel.at[1 - self.core, pl.ds(mod4(self.x + g) * 4, 4), self.rows(j)]
            self.arrived(("s", j, g), tiles, self.sib_recv.at[j, g % 4])

    def SQ(self, j, h):
        for d in (-1, 1, 2):
            for i in range(CHUNKS):
                self.y_arrived(0, h, d, i)
        if h == 1:
            for i in range(CHUNKS):
                self.y_arrived(0, 1, 0, i)
        for g in (-1, 1, 2):
            for o in range(4):
                self.x_arrived(g, j, o)
        self.sibling_arrived(j)
        zh = self.zh if h == 0 else 1 - self.zh

        def add(y, carry):
            total = None
            for t in range(4):
                left = self.panel[t % 2, (2 * zh + t // 2) * 4 + y, self.rows(j), :]
                right = self.p_cols[2 * y + zh, pl.ds(t * 256, 256), :]
                term = jnp.dot(left, right, preferred_element_type=jnp.float32)
                total = term if total is None else total + term
            self.square[self.rows(j), :] += total
            return carry

        lax.fori_loop(0, 4, add, 0)
        if h == 1:
            mine = 2 * self.y + self.zh
            for i, q, keep in self.flags(self.square_pattern, j):
                block = self.square[pl.ds(i * 128, 128), pl.ds(q * 128, 128)] * keep
                self.square[pl.ds(i * 128, 128), pl.ds(q * 128, 128)] = block
                self.s_cols[mine, pl.ds(i * 128, 128), pl.ds(q * 128, 128)] = block.astype(jnp.bfloat16)

    def CU(self, h, d, j):
        if (h, d) != (0, 0):
            self.y_arrived(1, h, d, j)
        zh = self.zh if h == 0 else 1 - self.zh
        y = mod4(self.y + d)
        t = j * self.step // 256
        width = min(self.step, 256)
        inner = pl.ds(j * self.step % 256, width)

        def add(i, carry):
            rows = pl.ds(pl.multiple_of(i * 256, 256), 256)
            left = self.panel[t % 2, (2 * zh + t // 2) * 4 + y, rows, inner]
            right = self.s_cols[2 * y + zh, self.rows(j), :]
            self.cube[rows, :] += jnp.dot(left, right, preferred_element_type=jnp.float32)
            return carry

        lax.fori_loop(0, 4, add, 0)

    def flags(self, pattern, j):
        base_row = (2 * self.y + self.zh) * 8
        base_col = ((self.zl * 4 + self.x) * 2 + self.core) * 2
        count = self.step // 128
        for i in range(j * count, (j + 1) * count):
            a = self.order[base_row + i]
            for q in range(2):
                b = self.order[base_col + q]
                kept = pattern[lax.min(a, b), lax.max(a, b)]
                yield i, q, jnp.where(kept > 0, jnp.float32(1), jnp.float32(0))

    def run(self):
        barrier = pltpu.get_barrier_semaphore()
        partners = [self.at_x(1), self.at_x(-1), self.at_y(1), self.at_y(-1), self.at_z(1), self.at_z(-1), self.at_z(2),
                    self.at_z(-2), self.at_z(4), self.other_core()]
        for device in partners:
            pl.semaphore_signal(barrier, inc=1, device_id=device, device_id_type=pl.DeviceIdType.MESH)
        mine, place = 2 * self.y + self.zh, self.x * 4 + self.zl
        for j in range(CHUNKS):
            for i, q, keep in self.flags(self.occupancy, j):
                block = self.p[pl.ds(i * 128, 128), pl.ds(q * 128, 128)].astype(jnp.float32) * keep
                block = block.astype(jnp.bfloat16)
                self.panel[self.core, place, pl.ds(i * 128, 128), pl.ds(q * 128, 128)] = block
                self.p_cols[mine, pl.ds(i * 128, 128), pl.ds(q * 128, 128)] = block
        self.square[...] = jnp.zeros_like(self.square)
        self.cube[...] = jnp.zeros_like(self.cube)
        pl.semaphore_wait(barrier, len(partners))
        for name, *args in ORDER:
            getattr(self, name)(*args)
        for j in range(CHUNKS):
            for i, q, keep in self.flags(self.cube_pattern, j):
                at = (pl.ds(i * 128, 128), pl.ds(q * 128, 128))
                self.out[at] = 3.0 * self.square[at] - 2.0 * (self.cube[at] * keep)
        for copy, guard in self.sent:
            if guard is None:
                copy.wait_send()
            else:
                pl.when(guard)(copy.wait_send)


def kernel(*refs):
    Step(refs).run()


def body(p_values, occupancy, square_pattern, cube_pattern, block_order):
    rows, cols = p_values.shape
    smem = pl.BlockSpec(memory_space=pltpu.SMEM)
    vmem = pl.BlockSpec(memory_space=pltpu.VMEM)
    sem = pltpu.SemaphoreType.DMA
    return pl.pallas_call(
        kernel,
        out_shape=jax.ShapeDtypeStruct((rows, cols), jnp.float32),
        in_specs=[smem] * 4 + [vmem],
        out_specs=vmem,
        scratch_shapes=[
            pltpu.VMEM((2, 16, rows, cols), jnp.bfloat16),
            pltpu.VMEM((8, rows, cols), jnp.bfloat16),
            pltpu.VMEM((8, rows, cols), jnp.bfloat16),
            pltpu.VMEM((rows, cols), jnp.float32),
            pltpu.VMEM((rows, cols), jnp.float32),
            sem((2, CHUNKS, 3)),
            sem((2, CHUNKS, 4)),
            sem((2, 2, CHUNKS, 2)),
            sem((2, 2, CHUNKS, 4)),
            sem((4, CHUNKS, 4)),
            sem((2, 2, 2, 2, CHUNKS)),
            sem((2, 2, 4, CHUNKS)),
            sem((CHUNKS, 4)),
            sem((CHUNKS, 4)),
        ],
        compiler_params=pltpu.CompilerParams(collective_id=0, has_side_effects=True, vmem_limit_bytes=48 * 2**20),
        cost_estimate=pl.CostEstimate(flops=4 * rows * cols * 8192, bytes_accessed=2**24, transcendentals=0),
    )(block_order, occupancy, square_pattern, cube_pattern, p_values)


def solution(mesh):
    finer = Mesh(mesh.devices.reshape(4, 2, 4, 4, 2), AXES)
    tiles = P(("y", "zh"), ("zl", "x", "core"))
    return jax.shard_map(
        body, mesh=finer, in_specs=(tiles, P(), P(), P(), P()), out_specs=tiles, check_vma=False
    )
```

```python
import functools
import jax
import jax.numpy as jnp
from jax import lax
from jax.experimental import pallas as pl
from jax.experimental.pallas import tpu as pltpu
from jax.sharding import Mesh
from jax.sharding import PartitionSpec as P

AXES = ("y", "zh", "zl", "x", "core")
CHUNKS = 8
X_FIRST = (7,)
SPAN = 2
SOURCES = (((0, 0), (0, -1), (0, 1)), ((1, 0), (0, 2)), ((1, -1), (1, 1)), ((1, 2),))
ORDER = (
    ("ZP", 4), ("X", -1, 0, 0), ("X", 1, 4, 0), ("Y", -1, 0, 0, 1), ("Y", -1, 0, 0, 3), ("X", -1, 2, 0), ("X", -1, 4, 0),
    ("Z", 1, 0), ("ZP", 1), ("X", 1, 5, 0), ("X", -1, 7, 0), ("Z", 4, 0), ("X", 1, 7, 0), ("X", 1, 1, 0), ("Z", 2, 0),
    ("X", -1, 3, 0), ("Z", 3, 0), ("ZP", 2), ("XF", 1, 4, 0), ("ZP", 3), ("Y", -1, 0, 0, 7), ("X", 1, 2, 0),
    ("Y", 1, 0, 0, 2), ("Y", 1, 0, 0, 6), ("Y", 1, 0, 0, 4), ("X", -1, 1, 0), ("Y", -1, 0, 0, 0), ("Z", 4, 1),
    ("YF", -1, 0, 0, 3), ("YF", -1, 0, 0, 7), ("Z", 2, 1), ("Y", 1, 0, 0, 7), ("Y", -1, 0, 0, 2), ("Y", -1, 0, 0, 5),
    ("YF", -1, 0, 0, 1), ("Z", 3, 1), ("X", -1, 2, 1), ("X", 1, 3, 0), ("X", -1, 4, 1), ("YF", 1, 0, 0, 2), ("Z", 4, 2),
    ("Z", 7, 0), ("X", 1, 3, 1), ("Z", 0, 0), ("Z", 2, 2), ("X", -1, 5, 0), ("Y", 1, 0, 0, 5), ("X", 1, 2, 1),
    ("X", -1, 2, 2), ("Y", -1, 0, 0, 4), ("ZP", 0), ("Y", 1, 0, 0, 0), ("Z", 1, 1), ("XF", 1, 3, 0), ("X", -1, 4, 2),
    ("Z", 3, 2), ("X", 1, 0, 0), ("Z", 4, 3), ("XF", 1, 2, 0), ("X", -1, 1, 1), ("Z", 2, 3), ("XH", -1, 7), ("X", -1, 2, 3),
    ("Z", 5, 0), ("X", 1, 2, 2), ("SIB", 4, 0), ("X", -1, 4, 3), ("ZP", 5), ("X", 1, 4, 1), ("XH", 1, 7), ("YF", 1, 0, 0, 0),
    ("Z", 3, 3), ("Z", 6, 0), ("Z", 1, 2), ("SIB", 2, 0), ("Z", 0, 1), ("YF", 1, 0, 0, 6), ("YF", 1, 0, 0, 4), ("X", 1, 3, 2),
    ("Y", -1, 0, 1, 2), ("Y", 1, 0, 1, 4), ("Y", -1, 0, 0, 6), ("Z", 5, 1), ("X", -1, 0, 1), ("X", -1, 3, 3), ("X", 1, 4, 3),
    ("Z", 1, 3), ("Z", 0, 2), ("X", 1, 2, 3), ("X", -1, 1, 2), ("X", 1, 3, 3), ("Z", 5, 2), ("SIB", 3, 0), ("X", 1, 4, 2),
    ("ZP", 6), ("Y", 1, 0, 1, 3), ("X", -1, 3, 2), ("X", 1, 0, 1), ("Y", -1, 0, 1, 1), ("X", -1, 0, 2), ("Y", 1, 0, 1, 2),
    ("Y", 1, 0, 0, 3), ("SIB", 1, 0), ("Z", 0, 3), ("X", -1, 0, 3), ("XF", -1, 2, 2), ("X", 1, 1, 1), ("Z", 5, 3),
    ("Y", -1, 0, 1, 3), ("Y", 1, 0, 0, 1), ("YF", 1, 0, 1, 4), ("SIB", 2, 1), ("ZP", 7), ("YF", -1, 0, 0, 5), ("X", 1, 0, 2),
    ("X", -1, 3, 1), ("XF", -1, 2, 3), ("XF", 1, 3, 1), ("XF", 1, 2, 1), ("SIB", 2, -1), ("X", -1, 1, 3), ("X", 1, 1, 2),
    ("Y", 1, 0, 1, 1), ("Z", 6, 1), ("Y", -1, 0, 1, 0), ("XF", -1, 3, 3), ("X", 1, 0, 3), ("YF", -1, 0, 1, 1), ("Z", 7, 1),
    ("XF", -1, 3, 2), ("YF", -1, 0, 1, 3), ("SIB", 0, 1), ("Z", 6, 2), ("YF", 1, 0, 1, 2), ("XF", 1, 0, 1), ("Z", 7, 2),
    ("XF", 1, 0, 0), ("SIB", 3, -1), ("XF", -1, 0, 2), ("Z", 6, 3), ("Y", -1, 0, 1, 5), ("XF", -1, 0, 3), ("Y", 1, 0, 1, 5),
    ("XF", 1, 4, 1), ("ZT", 2, 7, 0), ("XF", -1, 4, 3), ("XF", 1, 1, 1), ("SIB", 3, 1), ("ZT", -1, 7, 0), ("X", 1, 1, 3),
    ("Y", 1, 0, 1, 0), ("Z", 7, 3), ("XF", -1, 4, 2), ("ZT", 1, 7, 0), ("Y", -1, 0, 1, 4), ("X", 1, 5, 2), ("XF", 1, 1, 0),
    ("Y", -1, 0, 1, 6), ("SIB", 0, 0), ("SIB", 2, 2), ("Y", 1, 0, 1, 6), ("Y", -1, 0, 1, 7), ("ZT", 2, 7, 1), ("X", 1, 5, 1),
    ("X", 1, 6, 0), ("Y", 1, 0, 1, 7), ("ZT", -1, 7, 1), ("YF", -1, 0, 1, 5), ("SIB", 3, 2), ("SIB", 4, -1),
    ("YF", 1, 0, 1, 0), ("YF", 1, 0, 1, 6), ("SQ", 2, 0), ("ZT", 1, 7, 1), ("X", -1, 5, 3), ("X", 1, 5, 3), ("ZT", 2, 7, 2),
    ("XF", -1, 1, 3), ("YF", -1, 0, 1, 7), ("SIB", 7, 0), ("SQ", 3, 0), ("SIB", 1, 1), ("SIB", 0, -1), ("XF", -1, 1, 2),
    ("ZT", -1, 7, 2), ("X", -1, 6, 3), ("SIB", 0, 2), ("X", -1, 5, 2), ("X", -1, 6, 2), ("X", -1, 5, 1), ("SIB", 4, 1),
    ("SQ", 3, 1), ("X", 1, 6, 1), ("SQ", 2, 1), ("SIB", 4, 2), ("ZT", 1, 7, 2), ("SQ", 3, 2), ("ZT", 2, 7, 3),
    ("Y", -1, 1, 0, 3), ("Y", 1, 1, 0, 3), ("SQ", 2, 2), ("ES", 2), ("Y", 1, 1, 0, 2), ("SIB", 7, 2), ("Y", -1, 1, 0, 2),
    ("SQ", 0, 0), ("SQ", 0, 1), ("ZT", -1, 7, 3), ("SQ", 0, 2), ("Y", -1, 1, 0, 0), ("SIB", 7, -1), ("Y", 1, 1, 0, 0),
    ("ES", 3), ("ZT", 1, 7, 3), ("SIB", 7, 1), ("SQ", 4, 0), ("SQ", 4, 1), ("SQ", 4, 2), ("YF", -1, 1, 0, 3),
    ("Y", 1, 1, 0, 4), ("ES", 4), ("SIB", 1, -1), ("ES", 0), ("XF", 1, 5, 0), ("Y", -1, 1, 0, 4), ("YF", 1, 1, 0, 2),
    ("SIB", 1, 2), ("SQ", 7, 0), ("SQ", 7, 1), ("SQ", 7, 2), ("Y", -1, 1, 0, 7), ("XF", -1, 5, 3), ("Y", -1, 1, 1, 2),
    ("XF", -1, 5, 2), ("Y", 1, 1, 1, 2), ("SQ", 1, 0), ("XF", 1, 5, 1), ("YF", 1, 1, 0, 4), ("SQ", 1, 1), ("X", 1, 6, 2),
    ("SQ", 1, 2), ("X", -1, 6, 0), ("Y", 1, 1, 0, 7), ("ES", 1), ("SIB", 5, -1), ("Y", -1, 1, 0, 1), ("Y", -1, 1, 1, 3),
    ("YF", -1, 1, 0, 7), ("SIB", 5, 1), ("YF", 1, 1, 1, 2), ("SIB", 6, 0), ("X", 1, 6, 3), ("SIB", 5, 0), ("X", -1, 6, 1),
    ("XF", -1, 6, 2), ("XF", -1, 6, 3), ("SIB", 5, 2), ("Y", 1, 1, 1, 3), ("XF", 1, 6, 1), ("ES", 7), ("Y", -1, 1, 1, 4),
    ("Y", 1, 1, 0, 1), ("XF", 1, 6, 0), ("YF", -1, 1, 0, 1), ("SQ", 5, 0), ("Y", 1, 1, 1, 0), ("SQ", 5, 1), ("SIB", 6, -1),
    ("SQ", 5, 2), ("YF", 1, 1, 0, 0), ("SIB", 6, 1), ("Y", 1, 1, 0, 5), ("YF", -1, 1, 1, 3), ("ES", 5), ("SIB", 6, 2),
    ("Y", 1, 1, 1, 1), ("Y", -1, 1, 1, 0), ("Y", -1, 1, 0, 5), ("Y", -1, 1, 1, 1), ("Y", 1, 1, 1, 4), ("SQ", 6, 0),
    ("SQ", 6, 1), ("SQ", 6, 2), ("Y", -1, 1, 1, 7), ("ES", 6), ("CU", 2, 1), ("Y", 1, 1, 0, 6), ("CU", 1, 0),
    ("Y", 1, 1, 1, 7), ("CU", 1, 1), ("YF", -1, 1, 0, 5), ("CU", 3, 1), ("Y", -1, 1, 0, 6), ("Y", 1, 1, 1, 5),
    ("Y", -1, 1, 1, 5), ("CU", 0, 1), ("YF", 1, 1, 0, 6), ("YF", -1, 1, 1, 1), ("CU", 0, 0), ("CU", 0, 2), ("Y", 1, 1, 1, 6),
    ("CU", 1, 2), ("YF", 1, 1, 1, 0), ("Y", -1, 1, 1, 6), ("CU", 0, 3), ("CU", 2, 0), ("YF", -1, 1, 1, 5), ("YF", 1, 1, 1, 4),
    ("CU", 1, 3), ("CU", 2, 2), ("YF", -1, 1, 1, 7), ("YF", 1, 1, 1, 6), ("CU", 2, 3), ("CU", 3, 0), ("CU", 3, 2),
    ("CU", 3, 3),
)


def mod4(v):
    return lax.rem(v + 8, 4)


class Step:
    def __init__(self, refs):
        (self.order_in, self.occupancy_in, self.square_in, self.cube_in, self.p_in, self.out, self.order, self.occupancy,
         self.square_pattern, self.cube_pattern, self.panel, self.p_cols, self.s_cols, self.square, self.cube, self.in_sem,
         self.send_sem, self.z_recv, self.x_recv, self.y_recv, self.sib_recv) = refs
        self.y, self.zh, self.zl, self.x, self.core = (lax.axis_index(name) for name in AXES)
        self.step = self.panel.shape[2] // CHUNKS
        self.waited = set()
        pair = lax.rem(self.zl, 2)
        half = self.zl // 2
        self.places = (self.zl, self.zl + 1 - 2 * pair, 2 - half, 3 - 3 * half)

    def at_x(self, d):
        return {"x": mod4(self.x + d)}

    def at_y(self, d):
        return {"y": mod4(self.y + d)}

    def at_z(self, d):
        z = lax.rem(self.zh * 4 + self.zl + d + 8, 8)
        return {"zh": z // 4, "zl": lax.rem(z, 4)}

    def other_core(self):
        return {"core": 1 - self.core}

    def rows(self, j):
        return pl.ds(j * self.step, self.step)

    def half_rows(self, j, sign):
        return pl.ds(j * self.step + (0 if sign > 0 else self.step // 2), self.step // 2)

    def panel_at(self, g, zl, j):
        return self.panel.at[self.core, mod4(self.x + g) * 4 + zl, self.rows(j)]

    def half_at(self, g, j, sign):
        return self.panel.at[self.core, mod4(self.x + g) * 4 + self.zl, self.half_rows(j, sign)]

    def group(self, h, d):
        return 2 * mod4(self.y + d) + (self.zh if h == 0 else 1 - self.zh)

    def cols_at(self, phase, h, d, j):
        return (self.p_cols if phase == 0 else self.s_cols).at[self.group(h, d), self.rows(j)]

    def send(self, src, dst, kind, recv_sem, device, guard=None):
        copy = pltpu.make_async_remote_copy(
            src_ref=src, dst_ref=dst, send_sem=self.send_sem.at[kind], recv_sem=recv_sem, device_id=device,
            device_id_type=pl.DeviceIdType.MESH)
        if guard is None:
            copy.start()
        else:
            pl.when(guard)(copy.start)

    def arrived(self, key, dst, recv_sem, guard=None):
        if key in self.waited:
            return
        self.waited.add(key)
        copy = pltpu.make_async_remote_copy(
            src_ref=dst, dst_ref=dst, send_sem=recv_sem, recv_sem=recv_sem, device_id=self.other_core(),
            device_id_type=pl.DeviceIdType.MESH)
        if guard is None:
            copy.wait_recv()
        else:
            pl.when(guard)(copy.wait_recv)

    def sends_done(self, kind, tiles, rows, guard=None):
        part = self.panel.at[0, pl.ds(0, tiles), pl.ds(0, rows)]
        copy = pltpu.make_async_remote_copy(
            src_ref=part, dst_ref=part, send_sem=self.send_sem.at[kind], recv_sem=self.send_sem.at[kind],
            device_id=self.other_core(), device_id_type=pl.DeviceIdType.MESH)
        if guard is None:
            copy.wait_send()
        else:
            pl.when(guard)(copy.wait_send)

    def all_sends_done(self):
        step, first = self.step, len(X_FIRST)
        plain = CHUNKS - first
        end = (self.zl == 0) | (self.zl == 3)
        middle = (self.zl == 1) | (self.zl == 2)
        self.sends_done(0, plain, 8 * step)
        self.sends_done(1, plain, 4 * step)
        self.sends_done(2, 3, CHUNKS * step, end)
        self.sends_done(2, 5, CHUNKS * step, middle)
        self.sends_done(3, 6, CHUNKS * step)
        self.sends_done(4, 6, CHUNKS * step)
        self.sends_done(5, 1, CHUNKS * step)
        self.sends_done(6, 16, CHUNKS * step)
        if first:
            self.sends_done(7, 3 * first, step)
            self.sends_done(8, 3 * first, step, end)
            self.sends_done(8, 15 * first, step, middle)

    def x_arrived(self, g, j, o):
        self.arrived(("x", g, j, o), self.panel_at(g, self.places[o], j), self.x_recv.at[g % 4 - 1, j, o])

    def half_arrived(self, j, sign):
        self.arrived(("h", j, sign), self.half_at(2, j, sign), self.x_recv.at[1, j, (1 - sign) // 2])

    def group_arrived(self, g, j):
        if j not in X_FIRST:
            for o in range(4):
                self.x_arrived(g, j, o)
        elif g == 2:
            self.half_arrived(j, 1)
            self.half_arrived(j, -1)
        else:
            self.x_arrived(g, j, 0)

    def y_arrived(self, phase, h, d, j):
        self.arrived(("y", phase, h, d, j), self.cols_at(phase, h, d, j), self.y_recv.at[phase, h, d % 4, j])

    def line(self, g, j, d, kind, at):
        zl = self.zl
        low = self.panel_at(g, lax.max(zl - d, 0), j)
        high = self.panel_at(g, lax.min(zl + d, 3), j)
        if d > 0:
            self.arrived(("z", g, j, d, 0), low, self.z_recv.at[0, at, d - 1], zl >= d)
            self.arrived(("z", g, j, d, 1), high, self.z_recv.at[1, at, d - 1], zl <= 3 - d)
        if d < 3:
            self.send(low, low, kind, self.z_recv.at[0, at, d], self.at_z(1), (zl >= d) & (zl < 3))
            self.send(high, high, kind, self.z_recv.at[1, at, d], self.at_z(-1), (zl <= 3 - d) & (zl > 0))

    def Z(self, j, d):
        if d == 0:
            tile = self.panel_at(0, self.zl, j)
            self.send(tile, tile, 2, self.z_recv.at[0, j, 0], self.at_z(1), self.zl < 2)
            self.send(tile, tile, 2, self.z_recv.at[1, j, 0], self.at_z(-1), self.zl >= 2)
            return
        self.line(0, j, d, 2, j)
        if d >= 2:
            far = 4 - d
            mine = self.p_cols.at[self.group(0, 0), self.rows(j)]
            self.send(self.panel_at(0, 3 - d, j), mine, 2, self.y_recv.at[0, 1, 0, j], self.at_z(far), self.zl == 3)
            self.send(self.panel_at(0, d, j), mine, 2, self.y_recv.at[0, 1, 0, j], self.at_z(-far), self.zl == 0)

    def ZP(self, j):
        tile = self.panel_at(0, self.zl, j)
        self.send(tile, tile, 2, self.z_recv.at[1, j, 0], self.at_z(-1), self.zl == 1)
        self.send(tile, tile, 2, self.z_recv.at[0, j, 0], self.at_z(1), self.zl == 2)

    def ZT(self, g, j, d):
        if d == 0:
            self.group_arrived(g, j)
        self.line(g, j, d, 8, CHUNKS + 3 * X_FIRST.index(j) + g % 4 - 1)

    def X(self, sign, j, o):
        tile = self.panel_at(0, self.places[o], j)
        self.send(tile, tile, 7 if j in X_FIRST else 0, self.x_recv.at[-sign % 4 - 1, j, o], self.at_x(sign))

    def XF(self, sign, j, o):
        self.x_arrived(-sign, j, o)
        tile = self.panel_at(-sign, self.places[o], j)
        self.send(tile, tile, 1, self.x_recv.at[1, j, o], self.at_x(sign))

    def XH(self, sign, j):
        self.x_arrived(-sign, j, 0)
        tile = self.half_at(-sign, j, sign)
        self.send(tile, tile, 7, self.x_recv.at[1, j, (1 - sign) // 2], self.at_x(sign))

    def Y(self, sign, phase, h, j):
        if h == 1:
            self.y_arrived(phase, 1, 0, j)
        tile = self.cols_at(phase, h, 0, j)
        self.send(tile, tile, 3 + phase, self.y_recv.at[phase, h, -sign % 4, j], self.at_y(sign))

    def YF(self, sign, phase, h, j):
        self.y_arrived(phase, h, -sign, j)
        tile = self.cols_at(phase, h, -sign, j)
        self.send(tile, tile, 3 + phase, self.y_recv.at[phase, h, 2, j], self.at_y(sign))

    def ES(self, j):
        tile = self.cols_at(1, 0, 0, j)
        self.send(tile, tile, 5, self.y_recv.at[1, 1, 0, j], self.at_z(4))

    def SIB(self, j, g):
        if g != 0:
            self.group_arrived(g, j)
        tiles = self.panel.at[self.core, pl.ds(mod4(self.x + g) * 4, 4), self.rows(j)]
        self.send(tiles, tiles, 6, self.sib_recv.at[j, g % 4], self.other_core())

    def sibling_arrived(self, j):
        for g in (0, -1, 1, 2):
            tiles = self.panel.at[1 - self.core, pl.ds(mod4(self.x + g) * 4, 4), self.rows(j)]
            self.arrived(("s", j, g), tiles, self.sib_recv.at[j, g % 4])

    def square_terms(self, j, y, zh):
        total = None
        for t in range(4):
            left = self.panel[t % 2, (2 * zh + t // 2) * 4 + y, self.rows(j), :]
            right = self.p_cols[2 * y + zh, pl.ds(t * 256, 256), :]
            term = jnp.dot(left, right, preferred_element_type=jnp.float32)
            total = term if total is None else total + term
        return total

    def SQ(self, j, part):
        h = min(part, 1)
        for d in ((-1, 1, 2), (0, -1, 1), (2,))[part]:
            for i in range(CHUNKS):
                self.y_arrived(0, h, d, i)
        if part == 0:
            self.sibling_arrived(j)
        zh = self.zh if h == 0 else 1 - self.zh
        first, count = ((0, 4), (self.y - 1, 3), (self.y + 2, 1))[part]

        def add(i, carry):
            self.square[self.rows(j), :] += self.square_terms(j, mod4(first + i), zh)
            return carry

        lax.fori_loop(0, count, add, 0)
        if part == 2:
            mine = self.group(0, 0)
            for i, q, keep in self.flags(self.square_pattern, j):
                at = (pl.ds(i * 128, 128), pl.ds(q * 128, 128))
                block = self.square[at] * keep
                self.square[at] = block
                self.s_cols[(mine,) + at] = block.astype(jnp.bfloat16)

    def CU(self, sources, j):
        terms = []
        for h, d in SOURCES[sources]:
            for i in range(j * SPAN, (j + 1) * SPAN):
                if (h, d) != (0, 0):
                    self.y_arrived(1, h, d, i)
            terms.append((mod4(self.y + d), self.zh if h == 0 else 1 - self.zh))

        def add(i, carry):
            rows = pl.ds(pl.multiple_of(i * 256, 256), 256)
            total = None
            for y, zh in terms:
                left = self.panel[j % 2, (2 * zh + j // 2) * 4 + y, rows, :]
                right = self.s_cols[2 * y + zh, pl.ds(j * 256, 256), :]
                term = jnp.dot(left, right, preferred_element_type=jnp.float32)
                total = term if total is None else total + term
            self.cube[rows, :] += total
            return carry

        lax.fori_loop(0, 4, add, 0)

    def flags(self, pattern, j):
        base_row = self.group(0, 0) * 8
        base_col = ((self.zl * 4 + self.x) * 2 + self.core) * 2
        count = self.step // 128
        for i in range(j * count, (j + 1) * count):
            a = self.order[base_row + i]
            for q in range(2):
                b = self.order[base_col + q]
                kept = pattern[lax.min(a, b), lax.max(a, b)]
                yield i, q, jnp.where(kept > 0, jnp.float32(1), jnp.float32(0))

    def run(self):
        mine, place = self.group(0, 0), self.x * 4 + self.zl
        inputs = [
            pltpu.make_async_copy(src, dst, self.in_sem.at[i]) for i, (src, dst) in enumerate((
                (self.order_in, self.order), (self.occupancy_in, self.occupancy),
                (self.p_in, self.panel.at[self.core, place]),
                (self.square_in, self.square_pattern), (self.cube_in, self.cube_pattern)))]
        for copy in inputs:
            copy.start()
        barrier = pltpu.get_barrier_semaphore()
        partners = [self.at_x(1), self.at_x(-1), self.at_y(1), self.at_y(-1), self.at_z(1), self.at_z(-1), self.at_z(2),
                    self.at_z(-2), self.at_z(4), self.other_core()]
        for device in partners:
            pl.semaphore_signal(barrier, inc=1, device_id=device, device_id_type=pl.DeviceIdType.MESH)
        for copy in inputs:
            copy.wait()
        for j in range(CHUNKS):
            for i, q, keep in self.flags(self.occupancy, j):
                at = (pl.ds(i * 128, 128), pl.ds(q * 128, 128))
                block = (self.panel[(self.core, place) + at].astype(jnp.float32) * keep).astype(jnp.bfloat16)
                self.panel[(self.core, place) + at] = block
                self.p_cols[(mine,) + at] = block
        self.square[...] = jnp.zeros_like(self.square)
        self.cube[...] = jnp.zeros_like(self.cube)
        pl.semaphore_wait(barrier, len(partners))
        for name, *args in ORDER:
            getattr(self, name)(*args)
        for j in range(CHUNKS):
            for i, q, keep in self.flags(self.cube_pattern, j):
                at = (pl.ds(i * 128, 128), pl.ds(q * 128, 128))
                self.out[at] = 3.0 * self.square[at] - 2.0 * (self.cube[at] * keep)
        self.all_sends_done()


def kernel(*refs):
    Step(refs).run()


def body(p_values, occupancy, square_pattern, cube_pattern, block_order):
    rows, cols = p_values.shape
    hbm = pl.BlockSpec(memory_space=pltpu.HBM)
    sem = pltpu.SemaphoreType.DMA
    lines = CHUNKS + 3 * len(X_FIRST)
    return pl.pallas_call(
        kernel,
        out_shape=jax.ShapeDtypeStruct((rows, cols), jnp.float32),
        in_specs=[hbm] * 5,
        out_specs=pl.BlockSpec(memory_space=pltpu.VMEM),
        scratch_shapes=[
            pltpu.SMEM(block_order.shape, jnp.int32),
            pltpu.SMEM(occupancy.shape, jnp.int32),
            pltpu.SMEM(occupancy.shape, jnp.int32),
            pltpu.SMEM(occupancy.shape, jnp.int32),
            pltpu.VMEM((2, 16, rows, cols), jnp.bfloat16),
            pltpu.VMEM((8, rows, cols), jnp.bfloat16),
            pltpu.VMEM((8, rows, cols), jnp.bfloat16),
            pltpu.VMEM((rows, cols), jnp.float32),
            pltpu.VMEM((rows, cols), jnp.float32),
            sem((5,)),
            sem((9,)),
            sem((2, lines, 3)),
            sem((3, CHUNKS, 4)),
            sem((2, 2, 4, CHUNKS)),
            sem((CHUNKS, 4)),
        ],
        compiler_params=pltpu.CompilerParams(collective_id=0, has_side_effects=True, vmem_limit_bytes=48 * 2**20),
        cost_estimate=pl.CostEstimate(flops=4 * rows * cols * 8192, bytes_accessed=2**24, transcendentals=0),
    )(block_order, occupancy, square_pattern, cube_pattern, p_values)


def solution(mesh):
    finer = Mesh(mesh.devices.reshape(4, 2, 4, 4, 2), AXES)
    tiles = P(("y", "zh"), ("zl", "x", "core"))
    return jax.shard_map(
        body, mesh=finer, in_specs=(tiles, P(), P(), P(), P()), out_specs=tiles, check_vma=False
    )
```

```python
import functools
import jax
import jax.numpy as jnp
from jax import lax
from jax.experimental import pallas as pl
from jax.experimental.pallas import tpu as pltpu
from jax.sharding import Mesh
from jax.sharding import PartitionSpec as P

AXES = ("y", "zh", "zl", "x", "core")
CHUNKS = 8
X_FIRST = (7,)
SPAN = 2
SOURCES = (((0, 0), (0, -1), (0, 1)), ((1, 0), (0, 2)), ((1, -1), (1, 1)), ((1, 2),))
ORDER = (
    ("ZP", 2), ("X", 1, 7, 0), ("X", -1, 7, 0), ("ZP", 1), ("Z", 2, 0), ("X", -1, 3, 0), ("Y", -1, 0, 0, 6), ("Z", 1, 0),
    ("ZP", 0), ("Y", -1, 0, 0, 4), ("X", 1, 3, 0), ("Z", 0, 0), ("ZP", 4), ("Z", 4, 0), ("Y", -1, 0, 0, 5), ("Y", 1, 0, 0, 3),
    ("Y", -1, 0, 0, 1), ("X", -1, 0, 0), ("X", -1, 1, 0), ("X", 1, 2, 0), ("X", -1, 4, 0), ("Y", 1, 0, 0, 6), ("Z", 2, 1),
    ("Y", 1, 0, 0, 4), ("X", 1, 6, 0), ("X", 1, 0, 0), ("X", -1, 2, 1), ("Y", 1, 0, 0, 7), ("Z", 1, 1), ("X", 1, 1, 0),
    ("Z", 4, 1), ("Z", 3, 0), ("YF", 1, 0, 0, 4), ("X", -1, 2, 0), ("XF", 1, 2, 0), ("X", 1, 1, 1), ("YF", 1, 0, 0, 6),
    ("XH", -1, 7), ("Z", 2, 2), ("X", 1, 2, 1), ("X", -1, 2, 2), ("Y", -1, 0, 0, 3), ("Z", 1, 2), ("Z", 0, 1),
    ("YF", -1, 0, 0, 1), ("X", 1, 4, 1), ("X", -1, 1, 2), ("X", -1, 1, 1), ("Z", 5, 0), ("X", 1, 0, 1), ("Z", 4, 2),
    ("ZP", 3), ("Z", 2, 3), ("Y", -1, 0, 0, 7), ("XF", 1, 2, 1), ("X", -1, 2, 3), ("Y", 1, 0, 0, 1), ("SIB", 2, 0),
    ("Z", 1, 3), ("Z", 0, 2), ("XF", -1, 2, 2), ("Y", 1, 0, 1, 2), ("X", 1, 1, 2), ("Y", -1, 0, 1, 2), ("Y", 1, 0, 0, 5),
    ("Y", -1, 0, 0, 0), ("X", 1, 0, 2), ("Y", 1, 0, 0, 0), ("X", -1, 1, 3), ("X", -1, 4, 2), ("Z", 3, 1), ("Z", 6, 0),
    ("XF", -1, 2, 3), ("Z", 4, 3), ("XF", 1, 1, 1), ("X", -1, 0, 2), ("SIB", 1, 0), ("Z", 0, 3), ("YF", -1, 0, 0, 7),
    ("X", 1, 4, 0), ("ZP", 5), ("X", 1, 1, 3), ("X", -1, 4, 3), ("XH", 1, 7), ("Y", -1, 0, 1, 4), ("YF", -1, 0, 0, 5),
    ("Y", -1, 0, 1, 1), ("X", 1, 2, 3), ("Z", 3, 2), ("Y", 1, 0, 1, 1), ("Z", 3, 3), ("XF", -1, 1, 2), ("Y", 1, 0, 1, 4),
    ("XF", -1, 1, 3), ("ZP", 6), ("X", 1, 0, 3), ("XF", 1, 1, 0), ("Y", 1, 0, 0, 2), ("X", 1, 2, 2), ("Z", 7, 0),
    ("X", -1, 0, 3), ("X", 1, 3, 1), ("XF", 1, 0, 1), ("SIB", 2, 1), ("Z", 5, 1), ("Y", -1, 0, 0, 2), ("X", -1, 0, 1),
    ("YF", 1, 0, 0, 0), ("Z", 6, 1), ("Z", 5, 2), ("ZP", 7), ("Y", -1, 0, 1, 3), ("Y", 1, 0, 1, 0), ("SIB", 1, 1),
    ("X", -1, 3, 3), ("YF", -1, 0, 1, 1), ("Y", 1, 0, 1, 3), ("YF", 1, 0, 0, 2), ("X", 1, 4, 2), ("YF", -1, 0, 0, 3),
    ("Y", -1, 0, 1, 0), ("Z", 5, 3), ("XF", -1, 0, 2), ("XF", 1, 0, 0), ("SIB", 0, 0), ("SIB", 2, 2), ("X", 1, 4, 3),
    ("XF", 1, 4, 0), ("XF", -1, 4, 3), ("Z", 7, 1), ("Z", 6, 2), ("YF", 1, 0, 1, 4), ("XF", -1, 0, 3), ("XF", 1, 4, 1),
    ("X", 1, 3, 2), ("Z", 7, 2), ("ZT", -1, 7, 0), ("SIB", 3, 0), ("YF", -1, 0, 1, 3), ("X", 1, 6, 1), ("Z", 6, 3),
    ("YF", 1, 0, 1, 0), ("SIB", 6, 0), ("X", -1, 4, 1), ("X", -1, 3, 2), ("XF", -1, 4, 2), ("SIB", 0, -1), ("Z", 7, 3),
    ("Y", -1, 0, 1, 5), ("ZT", 1, 7, 0), ("Y", 1, 0, 1, 5), ("ZT", 2, 7, 0), ("X", 1, 3, 3), ("SIB", 7, 0), ("X", -1, 6, 2),
    ("XF", 1, 3, 1), ("SIB", 0, 1), ("XF", 1, 3, 0), ("XF", -1, 3, 3), ("SIB", 2, -1), ("SIB", 1, -1), ("Y", -1, 0, 1, 6),
    ("Y", 1, 0, 1, 6), ("SIB", 1, 2), ("Y", -1, 0, 1, 7), ("Y", 1, 0, 1, 7), ("YF", -1, 0, 1, 5), ("SQ", 2, 0),
    ("ZT", -1, 7, 1), ("YF", 1, 0, 1, 2), ("X", -1, 6, 3), ("X", -1, 3, 1), ("SQ", 1, 0), ("SIB", 0, 2), ("SIB", 4, 1),
    ("ZT", 1, 7, 1), ("X", 1, 6, 3), ("YF", 1, 0, 1, 6), ("SIB", 4, 0), ("YF", -1, 0, 1, 7), ("SIB", 4, -1), ("SQ", 2, 1),
    ("XF", -1, 3, 2), ("ZT", 2, 7, 1), ("SQ", 1, 1), ("X", -1, 6, 0), ("ZT", -1, 7, 2), ("X", -1, 6, 1), ("SQ", 0, 0),
    ("SIB", 4, 2), ("SQ", 0, 1), ("ZT", 1, 7, 2), ("SQ", 0, 2), ("Y", 1, 1, 0, 0), ("Y", -1, 1, 0, 0), ("SQ", 1, 2),
    ("ZT", -1, 7, 3), ("SIB", 7, -1), ("ZT", 2, 7, 2), ("SQ", 2, 2), ("ES", 0), ("Y", 1, 1, 0, 2), ("X", 1, 6, 2),
    ("Y", 1, 1, 0, 1), ("ES", 1), ("Y", -1, 1, 0, 1), ("XF", 1, 6, 1), ("ZT", 1, 7, 3), ("Y", -1, 1, 0, 2), ("SIB", 7, 1),
    ("SQ", 4, 0), ("ZT", 2, 7, 3), ("SIB", 7, 2), ("SQ", 4, 1), ("SQ", 4, 2), ("SIB", 3, -1), ("SIB", 3, 1), ("XF", -1, 6, 2),
    ("XF", -1, 6, 3), ("YF", 1, 1, 0, 0), ("Y", -1, 1, 0, 4), ("X", -1, 5, 2), ("XF", 1, 6, 0), ("X", 1, 5, 1),
    ("X", 1, 5, 0), ("ES", 2), ("SIB", 3, 2), ("Y", 1, 1, 0, 4), ("SQ", 7, 0), ("YF", -1, 1, 0, 1), ("SQ", 7, 1),
    ("SQ", 7, 2), ("YF", 1, 1, 0, 2), ("Y", 1, 1, 0, 7), ("Y", -1, 1, 0, 7), ("X", -1, 5, 3), ("SQ", 3, 0),
    ("Y", -1, 1, 1, 0), ("SIB", 6, 1), ("SQ", 3, 1), ("SIB", 6, -1), ("SQ", 3, 2), ("ES", 3), ("SIB", 6, 2), ("ES", 7),
    ("X", -1, 5, 1), ("Y", -1, 1, 0, 3), ("X", 1, 5, 2), ("Y", 1, 1, 0, 3), ("Y", 1, 1, 1, 0), ("XF", 1, 5, 1),
    ("YF", -1, 1, 0, 7), ("Y", -1, 1, 1, 1), ("X", -1, 5, 0), ("X", 1, 5, 3), ("XF", -1, 5, 2), ("YF", 1, 1, 0, 4),
    ("SQ", 6, 0), ("SIB", 5, 0), ("SQ", 6, 1), ("SQ", 6, 2), ("XF", -1, 5, 3), ("Y", 1, 1, 0, 6), ("ES", 6), ("XF", 1, 5, 0),
    ("YF", -1, 1, 0, 3), ("Y", -1, 1, 1, 2), ("ES", 4), ("Y", 1, 1, 1, 2), ("SIB", 5, 1), ("SIB", 5, -1), ("Y", 1, 1, 1, 1),
    ("YF", -1, 1, 1, 1), ("Y", -1, 1, 1, 3), ("SIB", 5, 2), ("Y", 1, 1, 1, 7), ("Y", -1, 1, 1, 7), ("Y", -1, 1, 0, 6),
    ("Y", 1, 1, 1, 3), ("YF", 1, 1, 0, 6), ("YF", 1, 1, 1, 0), ("SQ", 5, 0), ("SQ", 5, 1), ("SQ", 5, 2), ("ES", 5),
    ("Y", -1, 1, 1, 6), ("Y", 1, 1, 1, 6), ("CU", 1, 1), ("Y", 1, 1, 0, 5), ("CU", 2, 0), ("CU", 1, 0), ("Y", -1, 1, 1, 4),
    ("CU", 2, 1), ("Y", 1, 1, 1, 4), ("Y", -1, 1, 0, 5), ("CU", 0, 1), ("CU", 0, 3), ("Y", -1, 1, 1, 5), ("CU", 3, 0),
    ("Y", 1, 1, 1, 5), ("CU", 2, 3), ("YF", -1, 1, 1, 7), ("YF", 1, 1, 1, 6), ("CU", 1, 3), ("YF", -1, 1, 0, 5), ("CU", 0, 0),
    ("YF", 1, 1, 1, 4), ("YF", -1, 1, 1, 5), ("YF", 1, 1, 1, 2), ("CU", 0, 2), ("YF", -1, 1, 1, 3), ("CU", 2, 2),
    ("CU", 3, 3), ("CU", 1, 2), ("CU", 3, 2), ("CU", 3, 1),
)


def mod4(v):
    return lax.rem(v + 8, 4)


class Step:
    def __init__(self, refs):
        (self.order_in, self.occupancy_in, self.square_in, self.cube_in, self.p_in, self.out, self.order, self.occupancy,
         self.square_pattern, self.cube_pattern, self.panel, self.p_cols, self.s_cols, self.square, self.cube, self.in_sem,
         self.send_sem, self.z_recv, self.x_recv, self.far_recv, self.exchange_recv, self.pass_recv, self.y_recv,
         self.sib_recv) = refs
        self.y, self.zh, self.zl, self.x, self.core = (lax.axis_index(name) for name in AXES)
        self.step = self.panel.shape[2] // CHUNKS
        self.waited = set()
        pair = lax.rem(self.zl, 2)
        half = self.zl // 2
        self.places = (self.zl, self.zl + 1 - 2 * pair, 2 - half, 3 - 3 * half)

    def at_x(self, d):
        return {"x": mod4(self.x + d)}

    def at_y(self, d):
        return {"y": mod4(self.y + d)}

    def at_z(self, d):
        z = lax.rem(self.zh * 4 + self.zl + d + 8, 8)
        return {"zh": z // 4, "zl": lax.rem(z, 4)}

    def other_core(self):
        return {"core": 1 - self.core}

    def rows(self, j):
        return pl.ds(j * self.step, self.step)

    def half_rows(self, j, sign):
        return pl.ds(j * self.step + (0 if sign > 0 else self.step // 2), self.step // 2)

    def panel_at(self, g, zl, j):
        return self.panel.at[self.core, mod4(self.x + g) * 4 + zl, self.rows(j)]

    def half_at(self, g, j, sign):
        return self.panel.at[self.core, mod4(self.x + g) * 4 + self.zl, self.half_rows(j, sign)]

    def group(self, h, d):
        return 2 * mod4(self.y + d) + (self.zh if h == 0 else 1 - self.zh)

    def cols_at(self, phase, h, d, j):
        return (self.p_cols if phase == 0 else self.s_cols).at[self.group(h, d), self.rows(j)]

    def send(self, src, dst, kind, recv_sem, device, guard=None):
        copy = pltpu.make_async_remote_copy(
            src_ref=src, dst_ref=dst, send_sem=self.send_sem.at[kind], recv_sem=recv_sem, device_id=device,
            device_id_type=pl.DeviceIdType.MESH)
        if guard is None:
            copy.start()
        else:
            pl.when(guard)(copy.start)

    def arrived(self, key, dst, recv_sem, guard=None):
        if key in self.waited:
            return
        self.waited.add(key)
        copy = pltpu.make_async_remote_copy(
            src_ref=dst, dst_ref=dst, send_sem=recv_sem, recv_sem=recv_sem, device_id=self.other_core(),
            device_id_type=pl.DeviceIdType.MESH)
        if guard is None:
            copy.wait_recv()
        else:
            pl.when(guard)(copy.wait_recv)

    def sends_done(self, kind, tiles, rows, guard=None):
        part = self.panel.at[0, pl.ds(0, tiles), pl.ds(0, rows)]
        copy = pltpu.make_async_remote_copy(
            src_ref=part, dst_ref=part, send_sem=self.send_sem.at[kind], recv_sem=self.send_sem.at[kind],
            device_id=self.other_core(), device_id_type=pl.DeviceIdType.MESH)
        if guard is None:
            copy.wait_send()
        else:
            pl.when(guard)(copy.wait_send)

    def all_sends_done(self):
        step, first = self.step, len(X_FIRST)
        plain = CHUNKS - first
        end = (self.zl == 0) | (self.zl == 3)
        middle = (self.zl == 1) | (self.zl == 2)
        self.sends_done(0, plain, 8 * step)
        self.sends_done(1, plain, 4 * step)
        self.sends_done(2, 3, CHUNKS * step, end)
        self.sends_done(2, 5, CHUNKS * step, middle)
        self.sends_done(3, 6, CHUNKS * step)
        self.sends_done(4, 6, CHUNKS * step)
        self.sends_done(5, 1, CHUNKS * step)
        self.sends_done(6, 16, CHUNKS * step)
        if first:
            self.sends_done(7, 3 * first, step)
            self.sends_done(8, 3 * first, step, end)
            self.sends_done(8, 15 * first, step, middle)

    def x_arrived(self, g, j, o):
        self.arrived(("x", g, j, o), self.panel_at(g, self.places[o], j), self.x_sem(g, j, o))

    def x_sem(self, g, j, o):
        alone = o < 2 if g == -1 else o >= 2
        return self.x_recv.at[(g + 1) // 2, j, o % 2 if alone or j in X_FIRST else 2]

    def half_arrived(self, j, sign):
        self.arrived(("h", j, sign), self.half_at(2, j, sign), self.far_recv.at[j, (1 - sign) // 2])

    def group_arrived(self, g, j):
        if j not in X_FIRST and g == 2:
            tiles = self.panel.at[self.core, pl.ds(mod4(self.x + 2) * 4, 4), self.rows(j)]
            self.arrived(("g", j), tiles, self.far_recv.at[j, 0])
        elif j not in X_FIRST:
            for o in ((0, 1) if g == -1 else (2, 3)):
                self.x_arrived(g, j, o)
            pair = self.panel.at[self.core, pl.ds(0, 2), self.rows(j)]
            self.arrived(("p", g, j), pair, self.x_recv.at[(g + 1) // 2, j, 2])
        elif g == 2:
            self.half_arrived(j, 1)
            self.half_arrived(j, -1)
        else:
            self.x_arrived(g, j, 0)

    def passed_on(self, d, j):
        return d == (-1 if j % 2 == 0 else 1)

    def y_sem(self, phase, h, d, j):
        if d == 0:
            return self.exchange_recv.at[phase, j]
        if self.passed_on(d, j):
            return self.pass_recv.at[phase, h, j]
        return self.y_recv.at[h, int(d == 2), 0 if phase == 0 else 1 + j // SPAN]

    def y_arrived(self, phase, h, d, j):
        if d == 0 or self.passed_on(d, j):
            self.arrived(("y", phase, h, d, j), self.cols_at(phase, h, d, j), self.y_sem(phase, h, d, j))
        elif phase == 0:
            self.arrived(("late", 0, h, d == 2), self.p_cols.at[self.group(h, d)], self.y_sem(0, h, d, j))
        else:
            span = pl.ds(j // SPAN * 256, 256)
            self.arrived(("late", 1, h, d == 2, j // SPAN), self.s_cols.at[self.group(h, d), span], self.y_sem(1, h, d, j))

    def line(self, g, j, d, kind, at):
        zl = self.zl
        low = self.panel_at(g, lax.max(zl - d, 0), j)
        high = self.panel_at(g, lax.min(zl + d, 3), j)
        end = (zl == 0) | (zl == 3)
        if d == 1:
            both = self.panel.at[self.core, pl.ds(0, 2), self.rows(j)]
            self.arrived(("z", g, j, 1, 2), both, self.z_recv.at[at, 0], (zl == 1) | (zl == 2))
        if d in (1, 3):
            self.arrived(("z", g, j, d), low, self.z_recv.at[at, d - 1], end)
        elif d == 2:
            self.arrived(("z", g, j, 2), low, self.z_recv.at[at, 1])
        if d < 3:
            self.send(low, low, kind, self.z_recv.at[at, d], self.at_z(1), (zl >= d) & (zl < 3))
            self.send(high, high, kind, self.z_recv.at[at, d], self.at_z(-1), (zl <= 3 - d) & (zl > 0))

    def Z(self, j, d):
        if d == 0:
            tile = self.panel_at(0, self.zl, j)
            self.send(tile, tile, 2, self.z_recv.at[j, 0], self.at_z(1), self.zl < 2)
            self.send(tile, tile, 2, self.z_recv.at[j, 0], self.at_z(-1), self.zl >= 2)
            return
        self.line(0, j, d, 2, j)
        if d >= 2:
            far = 4 - d
            mine = self.p_cols.at[self.group(0, 0), self.rows(j)]
            self.send(self.panel_at(0, 3 - d, j), mine, 2, self.y_sem(0, 1, 0, j), self.at_z(far), self.zl == 3)
            self.send(self.panel_at(0, d, j), mine, 2, self.y_sem(0, 1, 0, j), self.at_z(-far), self.zl == 0)

    def ZP(self, j):
        tile = self.panel_at(0, self.zl, j)
        self.send(tile, tile, 2, self.z_recv.at[j, 0], self.at_z(-1), self.zl == 1)
        self.send(tile, tile, 2, self.z_recv.at[j, 0], self.at_z(1), self.zl == 2)

    def ZT(self, g, j, d):
        if d == 0:
            self.group_arrived(g, j)
        self.line(g, j, d, 8, CHUNKS + 3 * X_FIRST.index(j) + g % 4 - 1)

    def X(self, sign, j, o):
        tile = self.panel_at(0, self.places[o], j)
        self.send(tile, tile, 7 if j in X_FIRST else 0, self.x_sem(-sign, j, o), self.at_x(sign))

    def XF(self, sign, j, o):
        self.x_arrived(-sign, j, o)
        tile = self.panel_at(-sign, self.places[o], j)
        self.send(tile, tile, 1, self.far_recv.at[j, 0], self.at_x(sign))

    def XH(self, sign, j):
        self.x_arrived(-sign, j, 0)
        tile = self.half_at(-sign, j, sign)
        self.send(tile, tile, 7, self.far_recv.at[j, (1 - sign) // 2], self.at_x(sign))

    def Y(self, sign, phase, h, j):
        if h == 1:
            self.y_arrived(phase, 1, 0, j)
        tile = self.cols_at(phase, h, 0, j)
        self.send(tile, tile, 3 + phase, self.y_sem(phase, h, -sign, j), self.at_y(sign))

    def YF(self, sign, phase, h, j):
        self.y_arrived(phase, h, -sign, j)
        tile = self.cols_at(phase, h, -sign, j)
        self.send(tile, tile, 3 + phase, self.y_sem(phase, h, 2, j), self.at_y(sign))

    def ES(self, j):
        tile = self.cols_at(1, 0, 0, j)
        self.send(tile, tile, 5, self.y_sem(1, 1, 0, j), self.at_z(4))

    def SIB(self, j, g):
        if g != 0:
            self.group_arrived(g, j)
        tiles = self.panel.at[self.core, pl.ds(mod4(self.x + g) * 4, 4), self.rows(j)]
        self.send(tiles, tiles, 6, self.sib_recv.at[j], self.other_core())

    def sibling_arrived(self, j):
        self.arrived(("s", j), self.panel.at[1 - self.core, :, self.rows(j)], self.sib_recv.at[j])

    def square_terms(self, j, y, zh):
        total = None
        for t in range(4):
            left = self.panel[t % 2, (2 * zh + t // 2) * 4 + y, self.rows(j), :]
            right = self.p_cols[2 * y + zh, pl.ds(t * 256, 256), :]
            term = jnp.dot(left, right, preferred_element_type=jnp.float32)
            total = term if total is None else total + term
        return total

    def SQ(self, j, part):
        h = min(part, 1)
        for d in ((-1, 1, 2), (0, -1, 1), (2,))[part]:
            for i in range(CHUNKS):
                self.y_arrived(0, h, d, i)
        if part == 0:
            self.sibling_arrived(j)
        zh = self.zh if h == 0 else 1 - self.zh
        first, count = ((0, 4), (self.y - 1, 3), (self.y + 2, 1))[part]

        def add(i, carry):
            self.square[self.rows(j), :] += self.square_terms(j, mod4(first + i), zh)
            return carry

        lax.fori_loop(0, count, add, 0)
        if part == 2:
            mine = self.group(0, 0)
            for i, q, keep in self.flags(self.square_pattern, j):
                at = (pl.ds(i * 128, 128), pl.ds(q * 128, 128))
                block = self.square[at] * keep
                self.square[at] = block
                self.s_cols[(mine,) + at] = block.astype(jnp.bfloat16)

    def CU(self, sources, j):
        terms = []
        for h, d in SOURCES[sources]:
            for i in range(j * SPAN, (j + 1) * SPAN):
                if (h, d) != (0, 0):
                    self.y_arrived(1, h, d, i)
            terms.append((mod4(self.y + d), self.zh if h == 0 else 1 - self.zh))

        def add(i, carry):
            rows = pl.ds(pl.multiple_of(i * 256, 256), 256)
            total = None
            for y, zh in terms:
                left = self.panel[j % 2, (2 * zh + j // 2) * 4 + y, rows, :]
                right = self.s_cols[2 * y + zh, pl.ds(j * 256, 256), :]
                term = jnp.dot(left, right, preferred_element_type=jnp.float32)
                total = term if total is None else total + term
            self.cube[rows, :] += total
            return carry

        lax.fori_loop(0, 4, add, 0)

    def flags(self, pattern, j):
        base_row = self.group(0, 0) * 8
        base_col = ((self.zl * 4 + self.x) * 2 + self.core) * 2
        count = self.step // 128
        for i in range(j * count, (j + 1) * count):
            a = self.order[base_row + i]
            for q in range(2):
                b = self.order[base_col + q]
                kept = pattern[lax.min(a, b), lax.max(a, b)]
                yield i, q, jnp.where(kept > 0, jnp.float32(1), jnp.float32(0))

    def run(self):
        mine, place = self.group(0, 0), self.x * 4 + self.zl
        inputs = [
            pltpu.make_async_copy(src, dst, self.in_sem.at[i]) for i, (src, dst) in enumerate((
                (self.order_in, self.order), (self.occupancy_in, self.occupancy),
                (self.p_in, self.panel.at[self.core, place]),
                (self.square_in, self.square_pattern), (self.cube_in, self.cube_pattern)))]
        for copy in inputs:
            copy.start()
        barrier = pltpu.get_barrier_semaphore()
        partners = [self.at_x(1), self.at_x(-1), self.at_y(1), self.at_y(-1), self.at_z(1), self.at_z(-1), self.at_z(2),
                    self.at_z(-2), self.other_core()]
        for device in partners:
            pl.semaphore_signal(barrier, inc=1, device_id=device, device_id_type=pl.DeviceIdType.MESH)
        for copy in inputs:
            copy.wait()
        for j in range(CHUNKS):
            for i, q, keep in self.flags(self.occupancy, j):
                at = (pl.ds(i * 128, 128), pl.ds(q * 128, 128))
                block = (self.panel[(self.core, place) + at].astype(jnp.float32) * keep).astype(jnp.bfloat16)
                self.panel[(self.core, place) + at] = block
                self.p_cols[(mine,) + at] = block
        self.square[...] = jnp.zeros_like(self.square)
        self.cube[...] = jnp.zeros_like(self.cube)
        pl.semaphore_wait(barrier, len(partners))
        for name, *args in ORDER:
            getattr(self, name)(*args)
        for j in range(CHUNKS):
            for i, q, keep in self.flags(self.cube_pattern, j):
                at = (pl.ds(i * 128, 128), pl.ds(q * 128, 128))
                self.out[at] = 3.0 * self.square[at] - 2.0 * (self.cube[at] * keep)
        self.all_sends_done()


def kernel(*refs):
    Step(refs).run()


def body(p_values, occupancy, square_pattern, cube_pattern, block_order):
    rows, cols = p_values.shape
    hbm = pl.BlockSpec(memory_space=pltpu.HBM)
    sem = pltpu.SemaphoreType.DMA
    lines = CHUNKS + 3 * len(X_FIRST)
    return pl.pallas_call(
        kernel,
        out_shape=jax.ShapeDtypeStruct((rows, cols), jnp.float32),
        in_specs=[hbm] * 5,
        out_specs=pl.BlockSpec(memory_space=pltpu.VMEM),
        scratch_shapes=[
            pltpu.SMEM(block_order.shape, jnp.int32),
            pltpu.SMEM(occupancy.shape, jnp.int32),
            pltpu.SMEM(occupancy.shape, jnp.int32),
            pltpu.SMEM(occupancy.shape, jnp.int32),
            pltpu.VMEM((2, 16, rows, cols), jnp.bfloat16),
            pltpu.VMEM((8, rows, cols), jnp.bfloat16),
            pltpu.VMEM((8, rows, cols), jnp.bfloat16),
            pltpu.VMEM((rows, cols), jnp.float32),
            pltpu.VMEM((rows, cols), jnp.float32),
            sem((5,)),
            sem((9,)),
            sem((lines, 3)),
            sem((2, CHUNKS, 3)),
            sem((CHUNKS, 2)),
            sem((2, CHUNKS)),
            sem((2, 2, CHUNKS)),
            sem((2, 2, 5)),
            sem((CHUNKS,)),
        ],
        compiler_params=pltpu.CompilerParams(collective_id=0, has_side_effects=True, vmem_limit_bytes=48 * 2**20),
        cost_estimate=pl.CostEstimate(flops=4 * rows * cols * 8192, bytes_accessed=2**24, transcendentals=0),
    )(block_order, occupancy, square_pattern, cube_pattern, p_values)


def solution(mesh):
    finer = Mesh(mesh.devices.reshape(4, 2, 4, 4, 2), AXES)
    tiles = P(("y", "zh"), ("zl", "x", "core"))
    return jax.shard_map(
        body, mesh=finer, in_specs=(tiles, P(), P(), P(), P()), out_specs=tiles, check_vma=False
    )
```

```python
import functools
import jax
import jax.numpy as jnp
from jax import lax
from jax.experimental import pallas as pl
from jax.experimental.pallas import tpu as pltpu
from jax.sharding import Mesh
from jax.sharding import PartitionSpec as P

AXES = ("y", "zh", "zl", "x", "core")
CHUNKS = 8
X_FIRST = (2,)
SPAN = 2
LAST = 7
SOURCES = (((0, 0), (0, -1), (0, 1)), ((1, 0), (0, 2)), ((1, -1), (1, 1)), ((1, 2),))
ORDER = (
    ("ZP", 1), ("X", -1, 7, 0), ("X", 1, 0, 0), ("Z", 1, 0), ("Y", 1, 0, 0, 2), ("Y", -1, 0, 0, 5), ("X", 1, 4, 0),
    ("Y", -1, 0, 0, 6), ("Y", 1, 0, 0, 4), ("ZP", 4), ("X", 1, 1, 0), ("ZP", 0), ("X", -1, 4, 0), ("Z", 0, 0),
    ("Y", -1, 0, 0, 0), ("X", 1, 7, 0), ("X", -1, 1, 0), ("Y", 1, 0, 0, 3), ("Y", -1, 0, 0, 4), ("Z", 4, 0), ("X", -1, 2, 0),
    ("X", 1, 2, 0), ("Z", 1, 1), ("Y", 1, 0, 0, 6), ("Y", 1, 0, 0, 0), ("ZW", 1), ("Z", 0, 1), ("Z", 3, 0), ("X", -1, 5, 0),
    ("ZW", 4), ("X", -1, 0, 0), ("Y", -1, 0, 0, 3), ("X", -1, 1, 1), ("XF", 1, 0, 0), ("Z", 4, 1), ("XF", 1, 1, 0),
    ("Y", 1, 0, 0, 5), ("Z", 7, 0), ("Z", 1, 2), ("Y", -1, 0, 0, 1), ("Y", -1, 0, 0, 2), ("YF", 1, 0, 0, 6), ("X", 1, 1, 1),
    ("Y", -1, 0, 0, 7), ("X", -1, 4, 1), ("X", -1, 1, 2), ("Z", 0, 2), ("Y", 1, 0, 0, 1), ("YF", 1, 0, 0, 4), ("Z", 3, 1),
    ("X", -1, 3, 0), ("X", 1, 1, 2), ("X", 1, 4, 1), ("XF", 1, 4, 0), ("Z", 4, 2), ("Z", 2, 0), ("Z", 1, 3),
    ("YF", 1, 0, 0, 0), ("Z", 0, 3), ("X", -1, 0, 2), ("Y", -1, 0, 1, 1), ("SIB", 1, 0), ("X", -1, 4, 2), ("X", 1, 4, 2),
    ("Z", 7, 1), ("Z", 6, 0), ("X", -1, 0, 3), ("ZP", 3), ("X", 1, 6, 0), ("Z", 4, 3), ("X", 1, 4, 3), ("YF", -1, 0, 0, 5),
    ("X", -1, 4, 3), ("Y", 1, 0, 1, 0), ("YF", -1, 0, 0, 7), ("YF", -1, 0, 0, 1), ("YF", -1, 0, 0, 3), ("Z", 5, 0),
    ("X", 1, 1, 3), ("ZW", 0), ("X", -1, 1, 3), ("Z", 3, 2), ("Y", 1, 0, 0, 7), ("YF", -1, 0, 1, 1), ("XF", -1, 1, 2),
    ("Z", 7, 2), ("Y", 1, 0, 1, 4), ("YF", 1, 0, 1, 0), ("Z", 3, 3), ("XH", 1, 2), ("Z", 7, 3), ("Z", 2, 1), ("X", -1, 0, 1),
    ("XF", 1, 4, 1), ("X", 1, 0, 1), ("X", 1, 0, 3), ("ZW", 3), ("XF", 1, 1, 1), ("Z", 6, 1), ("XH", -1, 2), ("Z", 5, 1),
    ("X", 1, 0, 2), ("YF", 1, 0, 1, 4), ("Z", 2, 2), ("Y", -1, 0, 1, 3), ("XF", -1, 4, 3), ("Y", 1, 0, 1, 1), ("Z", 6, 2),
    ("Y", -1, 0, 1, 7), ("YF", 1, 0, 0, 2), ("XF", -1, 1, 3), ("XF", -1, 4, 2), ("Y", 1, 0, 1, 3), ("Y", -1, 0, 1, 0),
    ("Z", 5, 2), ("XF", 1, 7, 0), ("ZP", 7), ("ZP", 6), ("YF", -1, 0, 1, 3), ("X", 1, 3, 0), ("X", -1, 6, 2), ("Z", 2, 3),
    ("X", -1, 7, 2), ("ZT", -1, 2, 0), ("Y", -1, 0, 1, 4), ("YF", -1, 0, 1, 7), ("Z", 6, 3), ("Z", 5, 3), ("Y", 1, 0, 1, 2),
    ("XF", -1, 0, 2), ("SIB", 1, 1), ("ZW", 7), ("X", 1, 7, 1), ("XF", -1, 0, 3), ("ZT", 1, 2, 0), ("XF", 1, 0, 1), ("ZP", 5),
    ("SIB", 1, -1), ("Y", 1, 0, 1, 6), ("SIB", 4, -1), ("SIB", 7, 0), ("SIB", 1, 2), ("Y", 1, 0, 1, 7), ("ZT", 2, 2, 0),
    ("SIB", 4, 0), ("Y", -1, 0, 1, 5), ("YF", 1, 0, 1, 2), ("X", -1, 7, 1), ("X", 1, 6, 2), ("SIB", 0, 0), ("Y", 1, 0, 1, 5),
    ("Y", -1, 0, 1, 6), ("X", -1, 7, 3), ("X", 1, 7, 3), ("SIB", 4, 1), ("X", 1, 6, 3), ("ZP", 2), ("X", 1, 7, 2),
    ("SIB", 4, 2), ("Y", -1, 0, 1, 2), ("YF", 1, 0, 1, 6), ("ZW", 6), ("X", -1, 6, 1), ("ZT", -1, 2, 1), ("X", 1, 6, 1),
    ("X", 1, 3, 1), ("SQ", 1, 0), ("YF", -1, 0, 1, 5), ("XF", -1, 7, 2), ("SIB", 3, 0), ("X", -1, 6, 3), ("SIB", 0, 1),
    ("ZT", 1, 2, 1), ("XF", -1, 6, 2), ("SIB", 0, -1), ("XF", 1, 7, 1), ("SQ", 4, 0), ("SIB", 0, 2), ("SQ", 1, 1),
    ("SQ", 4, 1), ("SQ", 4, 2), ("SQ", 1, 2), ("XF", -1, 7, 3), ("ES", 1), ("Y", 1, 1, 0, 4), ("XF", 1, 6, 0), ("SQ", 0, 0),
    ("X", -1, 6, 0), ("SQ", 0, 1), ("SQ", 0, 2), ("SIB", 6, 0), ("ES", 4), ("ZT", 2, 2, 1), ("SIB", 7, -1), ("XF", 1, 6, 1),
    ("X", 1, 5, 0), ("XF", -1, 6, 3), ("ZW", 2), ("Y", -1, 1, 0, 4), ("Y", 1, 1, 0, 1), ("Y", 1, 1, 0, 0), ("X", -1, 3, 3),
    ("X", -1, 3, 2), ("X", -1, 3, 1), ("SIB", 7, 1), ("YF", 1, 1, 0, 4), ("SIB", 6, -1), ("ZT", -1, 2, 2), ("X", -1, 5, 3),
    ("Y", -1, 1, 0, 0), ("X", 1, 3, 2), ("ZT", 1, 2, 2), ("SIB", 7, 2), ("SX", 7, -1), ("Y", -1, 1, 0, 1), ("SX", 7, 0),
    ("Y", 1, 1, 1, 1), ("X", 1, 3, 3), ("SX", 7, 1), ("X", -1, 5, 2), ("SIB", 6, 1), ("SIB", 6, 2), ("SIB", 2, 0), ("ZW", 5),
    ("YF", 1, 1, 0, 0), ("SX", 7, 2), ("Y", -1, 1, 1, 1), ("XF", 1, 3, 1), ("Y", -1, 1, 1, 4), ("X", 1, 5, 3),
    ("ZT", 2, 2, 2), ("Y", -1, 1, 0, 7), ("ES", 7), ("Y", 1, 1, 0, 8), ("ZT", -1, 2, 3), ("Y", 1, 1, 1, 4), ("ES", 0),
    ("Y", 1, 1, 0, 7), ("X", 1, 5, 1), ("SIB", 2, -1), ("ZT", 1, 2, 3), ("XF", -1, 3, 3), ("YF", -1, 1, 0, 1), ("SIB", 2, 1),
    ("XF", 1, 3, 0), ("SQ", 6, 0), ("ZT", 2, 2, 3), ("SIB", 2, 2), ("SQ", 6, 1), ("SQ", 6, 2), ("Y", 1, 1, 0, 6),
    ("XF", -1, 3, 2), ("YF", -1, 1, 1, 1), ("SIB", 3, 1), ("X", 1, 5, 2), ("X", -1, 5, 1), ("ES", 8), ("XF", 1, 5, 0),
    ("XF", -1, 5, 3), ("ES", 6), ("YF", 1, 1, 0, 8), ("SIB", 3, -1), ("SQ", 2, 0), ("Y", -1, 1, 0, 6), ("YF", 1, 1, 1, 4),
    ("SQ", 2, 1), ("SQ", 2, 2), ("XF", -1, 5, 2), ("ES", 2), ("Y", -1, 1, 1, 7), ("Y", 1, 1, 0, 2), ("Y", -1, 1, 0, 2),
    ("XF", 1, 5, 1), ("SIB", 3, 2), ("Y", 1, 1, 1, 0), ("Y", 1, 1, 1, 8), ("YF", -1, 1, 0, 7), ("Y", 1, 1, 1, 7),
    ("SIB", 5, -1), ("SIB", 5, 1), ("Y", -1, 1, 1, 8), ("SIB", 5, 0), ("SQ", 3, 0), ("Y", -1, 1, 1, 0), ("YF", 1, 1, 0, 6),
    ("YF", -1, 1, 1, 7), ("SIB", 5, 2), ("SQ", 3, 1), ("SQ", 3, 2), ("Y", -1, 1, 1, 6), ("Y", -1, 1, 0, 3), ("Y", 1, 1, 1, 6),
    ("Y", 1, 1, 0, 3), ("YF", 1, 1, 1, 8), ("ES", 3), ("YF", 1, 1, 1, 0), ("SQ", 5, 0), ("SQ", 5, 1), ("SQ", 5, 2), ("ES", 5),
    ("Y", -1, 1, 0, 5), ("Y", -1, 1, 0, 8), ("CU", 1, 0), ("CU", 2, 0), ("Y", 1, 1, 0, 5), ("Y", -1, 1, 1, 2),
    ("YF", 1, 1, 1, 6), ("CU", 1, 3), ("Y", 1, 1, 1, 2), ("CU", 2, 3), ("YF", -1, 1, 0, 5), ("Y", 1, 1, 1, 3),
    ("Y", -1, 1, 1, 3), ("YF", 1, 1, 0, 2), ("CU", 3, 0), ("CU", 0, 0), ("CU", 0, 2), ("Y", -1, 1, 1, 5), ("YF", -1, 1, 0, 3),
    ("Y", 1, 1, 1, 5), ("CU", 3, 3), ("CU", 1, 2), ("YF", 1, 1, 1, 2), ("CU", 0, 3), ("YF", -1, 1, 1, 3), ("CU", 2, 1),
    ("YF", -1, 1, 1, 5), ("CU", 0, 1), ("CU", 1, 1), ("CU", 2, 2), ("CU", 3, 1), ("CU", 3, 2),
)


def mod4(v):
    return lax.rem(v + 8, 4)


class Step:
    def __init__(self, refs):
        (self.order_in, self.occupancy_in, self.square_in, self.cube_in, self.p_in, self.out, self.order, self.occupancy,
         self.square_pattern, self.cube_pattern, self.panel, self.p_cols, self.s_cols, self.square, self.cube, self.in_sem,
         self.send_sem, self.z_recv, self.x_recv, self.far_recv, self.exchange_recv, self.pass_recv, self.y_recv,
         self.sib_recv) = refs
        self.y, self.zh, self.zl, self.x, self.core = (lax.axis_index(name) for name in AXES)
        self.step = self.panel.shape[2] // CHUNKS
        self.waited = set()
        pair = lax.rem(self.zl, 2)
        half = self.zl // 2
        self.places = (self.zl, self.zl + 1 - 2 * pair, 2 - half, 3 - 3 * half)

    def at_x(self, d):
        return {"x": mod4(self.x + d)}

    def at_y(self, d):
        return {"y": mod4(self.y + d)}

    def at_z(self, d):
        z = lax.rem(self.zh * 4 + self.zl + d + 8, 8)
        return {"zh": z // 4, "zl": lax.rem(z, 4)}

    def other_core(self):
        return {"core": 1 - self.core}

    def rows(self, j):
        return pl.ds(j * self.step, self.step)

    def square_rows(self, j):
        if j not in (LAST, CHUNKS):
            return self.rows(j)
        return pl.ds(LAST * self.step + (self.step // 2 if j == CHUNKS else 0), self.step // 2)

    def half_rows(self, j, sign):
        return pl.ds(j * self.step + (0 if sign > 0 else self.step // 2), self.step // 2)

    def panel_at(self, g, zl, j):
        return self.panel.at[self.core, mod4(self.x + g) * 4 + zl, self.rows(j)]

    def half_at(self, g, j, sign):
        return self.panel.at[self.core, mod4(self.x + g) * 4 + self.zl, self.half_rows(j, sign)]

    def group(self, h, d):
        return 2 * mod4(self.y + d) + (self.zh if h == 0 else 1 - self.zh)

    def cols_at(self, phase, h, d, j):
        if phase == 0:
            return self.p_cols.at[self.group(h, d), self.rows(j)]
        return self.s_cols.at[self.group(h, d), self.square_rows(j)]

    def send(self, src, dst, kind, recv_sem, device, guard=None):
        copy = pltpu.make_async_remote_copy(
            src_ref=src, dst_ref=dst, send_sem=self.send_sem.at[kind], recv_sem=recv_sem, device_id=device,
            device_id_type=pl.DeviceIdType.MESH)
        if guard is None:
            copy.start()
        else:
            pl.when(guard)(copy.start)

    def arrived(self, key, dst, recv_sem, guard=None):
        if key in self.waited:
            return
        self.waited.add(key)
        copy = pltpu.make_async_remote_copy(
            src_ref=dst, dst_ref=dst, send_sem=recv_sem, recv_sem=recv_sem, device_id=self.other_core(),
            device_id_type=pl.DeviceIdType.MESH)
        if guard is None:
            copy.wait_recv()
        else:
            pl.when(guard)(copy.wait_recv)

    def sends_done(self, kind, tiles, rows, guard=None):
        part = self.panel.at[0, pl.ds(0, tiles), pl.ds(0, rows)]
        copy = pltpu.make_async_remote_copy(
            src_ref=part, dst_ref=part, send_sem=self.send_sem.at[kind], recv_sem=self.send_sem.at[kind],
            device_id=self.other_core(), device_id_type=pl.DeviceIdType.MESH)
        if guard is None:
            copy.wait_send()
        else:
            pl.when(guard)(copy.wait_send)

    def all_sends_done(self):
        step, first = self.step, len(X_FIRST)
        plain = CHUNKS - first
        end = (self.zl == 0) | (self.zl == 3)
        middle = (self.zl == 1) | (self.zl == 2)
        self.sends_done(0, plain, 8 * step)
        self.sends_done(1, plain, 4 * step)
        self.sends_done(2, 3, CHUNKS * step, end)
        self.sends_done(2, 5, CHUNKS * step, middle)
        self.sends_done(3, 6, CHUNKS * step)
        self.sends_done(4, 6, CHUNKS * step)
        self.sends_done(5, 1, CHUNKS * step)
        self.sends_done(6, 16, CHUNKS * step)
        if first:
            self.sends_done(7, 3 * first, step)
            self.sends_done(8, 3 * first, step, end)
            self.sends_done(8, 15 * first, step, middle)

    def x_arrived(self, g, j, o):
        self.arrived(("x", g, j, o), self.panel_at(g, self.places[o], j), self.x_sem(g, j, o))

    def x_sem(self, g, j, o):
        alone = o < 2 if g == -1 else o >= 2
        return self.x_recv.at[(g + 1) // 2, j, o % 2 if alone or j in X_FIRST else 2]

    def half_arrived(self, j, sign):
        self.arrived(("h", j, sign), self.half_at(2, j, sign), self.far_recv.at[j, (1 - sign) // 2])

    def group_arrived(self, g, j):
        if j not in X_FIRST and g == 2:
            tiles = self.panel.at[self.core, pl.ds(mod4(self.x + 2) * 4, 4), self.rows(j)]
            self.arrived(("g", j), tiles, self.far_recv.at[j, 0])
        elif j not in X_FIRST:
            for o in ((0, 1) if g == -1 else (2, 3)):
                self.x_arrived(g, j, o)
            pair = self.panel.at[self.core, pl.ds(0, 2), self.rows(j)]
            self.arrived(("p", g, j), pair, self.x_recv.at[(g + 1) // 2, j, 2])
        elif g == 2:
            self.half_arrived(j, 1)
            self.half_arrived(j, -1)
        else:
            self.x_arrived(g, j, 0)

    def passed_on(self, d, j):
        return d == (-1 if j % 2 == 0 else 1)

    def span(self, j):
        return (LAST if j == CHUNKS else j) // SPAN

    def y_sem(self, phase, h, d, j):
        if d == 0:
            return self.exchange_recv.at[phase, j]
        if self.passed_on(d, j):
            return self.pass_recv.at[phase, h, j]
        return self.y_recv.at[h, int(d == 2), 0 if phase == 0 else 1 + self.span(j)]

    def y_arrived(self, phase, h, d, j):
        if d == 0 or self.passed_on(d, j):
            self.arrived(("y", phase, h, d, j), self.cols_at(phase, h, d, j), self.y_sem(phase, h, d, j))
        elif phase == 0:
            self.arrived(("late", 0, h, d == 2), self.p_cols.at[self.group(h, d)], self.y_sem(0, h, d, j))
        else:
            span = self.span(j)
            part = self.s_cols.at[self.group(h, d), pl.ds(span * 256, 256)]
            self.arrived(("late", 1, h, d == 2, span), part, self.y_sem(1, h, d, j))

    def line(self, g, j, d, kind, at):
        zl = self.zl
        low = self.panel_at(g, lax.max(zl - d, 0), j)
        high = self.panel_at(g, lax.min(zl + d, 3), j)
        end = (zl == 0) | (zl == 3)
        if d == 1:
            both = self.panel.at[self.core, pl.ds(0, 2), self.rows(j)]
            self.arrived(("z", g, j, 1, 2), both, self.z_recv.at[at, 0], (zl == 1) | (zl == 2))
        if d == 3 or d == 1 and g != 0:
            self.arrived(("z", g, j, d), low, self.z_recv.at[at, d - 1], end)
        elif d == 2:
            self.arrived(("z", g, j, 2), low, self.z_recv.at[at, 1])
        if d < 3:
            self.send(low, low, kind, self.z_recv.at[at, d], self.at_z(1), (zl >= d) & (zl < 3))
            self.send(high, high, kind, self.z_recv.at[at, d], self.at_z(-1), (zl <= 3 - d) & (zl > 0))

    def Z(self, j, d):
        if d == 0:
            tile = self.panel_at(0, self.zl, j)
            self.send(tile, tile, 2, self.z_recv.at[j, 0], self.at_z(1), self.zl < 2)
            self.send(tile, tile, 2, self.z_recv.at[j, 0], self.at_z(-1), self.zl >= 2)
            return
        self.line(0, j, d, 2, j)
        if d >= 2:
            far = 4 - d
            mine = self.p_cols.at[self.group(0, 0), self.rows(j)]
            self.send(self.panel_at(0, 3 - d, j), mine, 2, self.y_sem(0, 1, 0, j), self.at_z(far), self.zl == 3)
            self.send(self.panel_at(0, d, j), mine, 2, self.y_sem(0, 1, 0, j), self.at_z(-far), self.zl == 0)

    def ZW(self, j):
        end = (self.zl == 0) | (self.zl == 3)
        self.arrived(("z", 0, j, 1), self.panel_at(0, self.places[1], j), self.z_recv.at[j, 0], end)

    def ZP(self, j):
        tile = self.panel_at(0, self.zl, j)
        self.send(tile, tile, 2, self.z_recv.at[j, 0], self.at_z(-1), self.zl == 1)
        self.send(tile, tile, 2, self.z_recv.at[j, 0], self.at_z(1), self.zl == 2)

    def ZT(self, g, j, d):
        if d == 0:
            self.group_arrived(g, j)
        self.line(g, j, d, 8, CHUNKS + 3 * X_FIRST.index(j) + g % 4 - 1)

    def X(self, sign, j, o):
        tile = self.panel_at(0, self.places[o], j)
        self.send(tile, tile, 7 if j in X_FIRST else 0, self.x_sem(-sign, j, o), self.at_x(sign))

    def XF(self, sign, j, o):
        self.x_arrived(-sign, j, o)
        tile = self.panel_at(-sign, self.places[o], j)
        self.send(tile, tile, 1, self.far_recv.at[j, 0], self.at_x(sign))

    def XH(self, sign, j):
        self.x_arrived(-sign, j, 0)
        tile = self.half_at(-sign, j, sign)
        self.send(tile, tile, 7, self.far_recv.at[j, (1 - sign) // 2], self.at_x(sign))

    def Y(self, sign, phase, h, j):
        if h == 1:
            self.y_arrived(phase, 1, 0, j)
        tile = self.cols_at(phase, h, 0, j)
        self.send(tile, tile, 3 + phase, self.y_sem(phase, h, -sign, j), self.at_y(sign))

    def YF(self, sign, phase, h, j):
        self.y_arrived(phase, h, -sign, j)
        tile = self.cols_at(phase, h, -sign, j)
        self.send(tile, tile, 3 + phase, self.y_sem(phase, h, 2, j), self.at_y(sign))

    def ES(self, j):
        tile = self.cols_at(1, 0, 0, j)
        self.send(tile, tile, 5, self.y_sem(1, 1, 0, j), self.at_z(4))

    def SIB(self, j, g):
        if g != 0:
            self.group_arrived(g, j)
        tiles = self.panel.at[self.core, pl.ds(mod4(self.x + g) * 4, 4), self.rows(j)]
        self.send(tiles, tiles, 6, self.sib_recv.at[CHUNKS + g % 4 if j == LAST else j],
                  self.other_core())

    def sibling_arrived(self, j):
        self.arrived(("s", j), self.panel.at[1 - self.core, :, self.rows(j)], self.sib_recv.at[j])

    def sibling_group_arrived(self, j, g):
        tiles = self.panel.at[1 - self.core, pl.ds(mod4(self.x + g) * 4, 4), self.rows(j)]
        self.arrived(("sg", j, g), tiles, self.sib_recv.at[CHUNKS + g % 4])

    def square_terms(self, j, y, zh):
        total = None
        for t in range(4):
            left = self.panel[t % 2, (2 * zh + t // 2) * 4 + y, self.rows(j), :]
            right = self.p_cols[2 * y + zh, pl.ds(t * 256, 256), :]
            term = jnp.dot(left, right, preferred_element_type=jnp.float32)
            total = term if total is None else total + term
        return total

    def SQ(self, j, part):
        h = min(part, 1)
        for d in ((-1, 1, 2), (0, -1, 1), (2,))[part]:
            for i in range(CHUNKS):
                self.y_arrived(0, h, d, i)
        if part == 0:
            self.sibling_arrived(j)
        zh = self.zh if h == 0 else 1 - self.zh
        first, count = ((0, 4), (self.y - 1, 3), (self.y + 2, 1))[part]

        def add(i, carry):
            self.square[self.rows(j), :] += self.square_terms(j, mod4(first + i), zh)
            return carry

        lax.fori_loop(0, count, add, 0)
        if part == 2:
            self.keep_square(j)

    def SX(self, j, g):
        for h in (0, 1):
            for d in (0, -1, 1, 2):
                for i in range(CHUNKS):
                    if (h, d) != (0, 0):
                        self.y_arrived(0, h, d, i)
        if g != 0:
            self.group_arrived(g, j)
        self.sibling_group_arrived(j, g)
        x = mod4(self.x + g)
        zh, pair = x // 2, lax.rem(x, 2)

        def add(zl, carry):
            total = None
            for core in range(2):
                left = self.panel[core, x * 4 + zl, self.rows(j), :]
                right = self.p_cols[2 * zl + zh, pl.ds(pl.multiple_of((2 * pair + core) * 256, 256), 256), :]
                term = jnp.dot(left, right, preferred_element_type=jnp.float32)
                total = term if total is None else total + term
            self.square[self.rows(j), :] += total
            return carry

        lax.fori_loop(0, 4, add, 0)
        if g == 2:
            self.keep_square(j)

    def keep_square(self, j):
        mine = self.group(0, 0)
        for i, q, keep in self.flags(self.square_pattern, j):
            at = (pl.ds(i * 128, 128), pl.ds(q * 128, 128))
            block = self.square[at] * keep
            self.square[at] = block
            self.s_cols[(mine,) + at] = block.astype(jnp.bfloat16)

    def CU(self, sources, j, last=False):
        terms = []
        parts = list(range(j * SPAN, (j + 1) * SPAN)) + ([CHUNKS] if LAST // SPAN == j else [])
        for h, d in SOURCES[sources]:
            for i in parts:
                if (h, d) != (0, 0):
                    self.y_arrived(1, h, d, i)
            terms.append((mod4(self.y + d), self.zh if h == 0 else 1 - self.zh))

        def add(i, carry):
            rows = pl.ds(pl.multiple_of(i * 256, 256), 256)
            total = None
            for y, zh in terms:
                left = self.panel[j % 2, (2 * zh + j // 2) * 4 + y, rows, :]
                right = self.s_cols[2 * y + zh, pl.ds(j * 256, 256), :]
                term = jnp.dot(left, right, preferred_element_type=jnp.float32)
                total = term if total is None else total + term
            if last:
                total += self.cube[rows, :]
                for r in range(2):
                    for q in range(2):
                        at = (pl.ds(pl.multiple_of(i * 256 + r * 128, 128), 128), pl.ds(q * 128, 128))
                        block = total[r * 128:(r + 1) * 128, q * 128:(q + 1) * 128]
                        self.out[at] = 3.0 * self.square[at] - 2.0 * (block * self.flag(self.cube_pattern, 2 * i + r, q))
            else:
                self.cube[rows, :] += total
            return carry

        lax.fori_loop(0, 4, add, 0)

    def flag(self, pattern, i, q):
        a = self.order[self.group(0, 0) * 8 + i]
        b = self.order[((self.zl * 4 + self.x) * 2 + self.core) * 2 + q]
        kept = pattern[lax.min(a, b), lax.max(a, b)]
        return jnp.where(kept > 0, jnp.float32(1), jnp.float32(0))

    def flags(self, pattern, j):
        count = self.step // 128
        for i in range(j * count, (j + 1) * count):
            for q in range(2):
                yield i, q, self.flag(pattern, i, q)

    def run(self):
        mine, place = self.group(0, 0), self.x * 4 + self.zl
        inputs = [
            pltpu.make_async_copy(src, dst, self.in_sem.at[i]) for i, (src, dst) in enumerate((
                (self.order_in, self.order), (self.occupancy_in, self.occupancy),
                (self.p_in, self.panel.at[self.core, place]),
                (self.square_in, self.square_pattern), (self.cube_in, self.cube_pattern)))]
        for copy in inputs:
            copy.start()
        barrier = pltpu.get_barrier_semaphore()
        partners = [self.at_x(1), self.at_x(-1), self.at_y(1), self.at_y(-1), self.at_z(1), self.at_z(-1), self.at_z(2),
                    self.at_z(-2), self.other_core()]
        for device in partners:
            pl.semaphore_signal(barrier, inc=1, device_id=device, device_id_type=pl.DeviceIdType.MESH)
        for copy in inputs:
            copy.wait()
        for j in range(CHUNKS):
            for i, q, keep in self.flags(self.occupancy, j):
                at = (pl.ds(i * 128, 128), pl.ds(q * 128, 128))
                block = (self.panel[(self.core, place) + at].astype(jnp.float32) * keep).astype(jnp.bfloat16)
                self.panel[(self.core, place) + at] = block
                self.p_cols[(mine,) + at] = block
        self.square[...] = jnp.zeros_like(self.square)
        self.cube[...] = jnp.zeros_like(self.cube)
        pl.semaphore_wait(barrier, len(partners))
        for name, *args in ORDER[:-1]:
            getattr(self, name)(*args)
        self.CU(*ORDER[-1][1:], last=True)
        self.all_sends_done()


def kernel(*refs):
    Step(refs).run()


def body(p_values, occupancy, square_pattern, cube_pattern, block_order):
    rows, cols = p_values.shape
    hbm = pl.BlockSpec(memory_space=pltpu.HBM)
    sem = pltpu.SemaphoreType.DMA
    lines = CHUNKS + 3 * len(X_FIRST)
    return pl.pallas_call(
        kernel,
        out_shape=jax.ShapeDtypeStruct((rows, cols), jnp.float32),
        in_specs=[hbm] * 5,
        out_specs=pl.BlockSpec(memory_space=pltpu.VMEM),
        scratch_shapes=[
            pltpu.SMEM(block_order.shape, jnp.int32),
            pltpu.SMEM(occupancy.shape, jnp.int32),
            pltpu.SMEM(occupancy.shape, jnp.int32),
            pltpu.SMEM(occupancy.shape, jnp.int32),
            pltpu.VMEM((2, 16, rows, cols), jnp.bfloat16),
            pltpu.VMEM((8, rows, cols), jnp.bfloat16),
            pltpu.VMEM((8, rows, cols), jnp.bfloat16),
            pltpu.VMEM((rows, cols), jnp.float32),
            pltpu.VMEM((rows, cols), jnp.float32),
            sem((5,)),
            sem((9,)),
            sem((lines, 3)),
            sem((2, CHUNKS, 3)),
            sem((CHUNKS, 2)),
            sem((2, CHUNKS + 1)),
            sem((2, 2, CHUNKS + 1)),
            sem((2, 2, 5)),
            sem((CHUNKS + 4,)),
        ],
        compiler_params=pltpu.CompilerParams(collective_id=0, has_side_effects=True, vmem_limit_bytes=48 * 2**20),
        cost_estimate=pl.CostEstimate(flops=4 * rows * cols * 8192, bytes_accessed=2**24, transcendentals=0),
    )(block_order, occupancy, square_pattern, cube_pattern, p_values)


def solution(mesh):
    finer = Mesh(mesh.devices.reshape(4, 2, 4, 4, 2), AXES)
    tiles = P(("y", "zh"), ("zl", "x", "core"))
    return jax.shard_map(
        body, mesh=finer, in_specs=(tiles, P(), P(), P(), P()), out_specs=tiles, check_vma=False
    )
```

```python
import functools
import jax
import jax.numpy as jnp
from jax import lax
from jax.experimental import pallas as pl
from jax.experimental.pallas import tpu as pltpu
from jax.sharding import Mesh
from jax.sharding import PartitionSpec as P

AXES = ("y", "zh", "zl", "x", "core")
CHUNKS = 8
X_FIRST = (2,)
SPAN = 2
LAST = 7
SOURCES = (((0, 0), (0, -1), (0, 1)), ((1, 0), (0, 2)), ((1, -1), (1, 1)), ((1, 2),))
ORDER = (
    ("ZP", 1), ("X", -1, 7, 0), ("X", 1, 0, 0), ("Z", 1, 0), ("Y", 1, 0, 0, 2), ("Y", -1, 0, 0, 5), ("X", 1, 4, 0),
    ("Y", -1, 0, 0, 6), ("Y", 1, 0, 0, 4), ("ZP", 4), ("X", 1, 1, 0), ("ZP", 0), ("X", -1, 4, 0), ("Z", 0, 0),
    ("Y", -1, 0, 0, 0), ("X", 1, 7, 0), ("X", -1, 1, 0), ("Y", 1, 0, 0, 3), ("Y", -1, 0, 0, 4), ("Z", 4, 0), ("X", -1, 2, 0),
    ("X", 1, 2, 0), ("Z", 1, 1), ("Y", 1, 0, 0, 6), ("Y", 1, 0, 0, 0), ("ZW", 1), ("Z", 0, 1), ("Z", 3, 0), ("X", -1, 5, 0),
    ("ZW", 4), ("X", -1, 0, 0), ("Y", -1, 0, 0, 3), ("X", -1, 1, 1), ("XF", 1, 0, 0), ("Z", 4, 1), ("XF", 1, 1, 0),
    ("Y", 1, 0, 0, 5), ("Z", 7, 0), ("Z", 1, 2), ("Y", -1, 0, 0, 1), ("Y", -1, 0, 0, 2), ("YF", 1, 0, 0, 6), ("X", 1, 1, 1),
    ("Y", -1, 0, 0, 7), ("X", -1, 4, 1), ("X", -1, 1, 2), ("Z", 0, 2), ("Y", 1, 0, 0, 1), ("YF", 1, 0, 0, 4), ("Z", 3, 1),
    ("X", -1, 3, 0), ("X", 1, 1, 2), ("X", 1, 4, 1), ("XF", 1, 4, 0), ("Z", 4, 2), ("Z", 2, 0), ("Z", 1, 3),
    ("YF", 1, 0, 0, 0), ("Z", 0, 3), ("X", -1, 0, 2), ("Y", -1, 0, 1, 1), ("SIB", 1, 0), ("X", -1, 4, 2), ("X", 1, 4, 2),
    ("Z", 7, 1), ("Z", 6, 0), ("X", -1, 0, 3), ("ZP", 3), ("X", 1, 6, 0), ("Z", 4, 3), ("X", 1, 4, 3), ("YF", -1, 0, 0, 5),
    ("X", -1, 4, 3), ("Y", 1, 0, 1, 0), ("YF", -1, 0, 0, 7), ("YF", -1, 0, 0, 1), ("YF", -1, 0, 0, 3), ("Z", 5, 0),
    ("X", 1, 1, 3), ("ZW", 0), ("X", -1, 1, 3), ("Z", 3, 2), ("Y", 1, 0, 0, 7), ("YF", -1, 0, 1, 1), ("XF", -1, 1, 2),
    ("Z", 7, 2), ("Y", 1, 0, 1, 4), ("YF", 1, 0, 1, 0), ("Z", 3, 3), ("XH", 1, 2), ("Z", 7, 3), ("Z", 2, 1), ("X", -1, 0, 1),
    ("XF", 1, 4, 1), ("X", 1, 0, 1), ("X", 1, 0, 3), ("ZW", 3), ("XF", 1, 1, 1), ("Z", 6, 1), ("XH", -1, 2), ("Z", 5, 1),
    ("X", 1, 0, 2), ("YF", 1, 0, 1, 4), ("Z", 2, 2), ("Y", -1, 0, 1, 3), ("XF", -1, 4, 3), ("Y", 1, 0, 1, 1), ("Z", 6, 2),
    ("Y", -1, 0, 1, 7), ("YF", 1, 0, 0, 2), ("XF", -1, 1, 3), ("XF", -1, 4, 2), ("Y", 1, 0, 1, 3), ("Y", -1, 0, 1, 0),
    ("Z", 5, 2), ("XF", 1, 7, 0), ("ZP", 7), ("ZP", 6), ("YF", -1, 0, 1, 3), ("X", 1, 3, 0), ("X", -1, 6, 2), ("Z", 2, 3),
    ("X", -1, 7, 2), ("ZT", -1, 2, 0), ("Y", -1, 0, 1, 4), ("YF", -1, 0, 1, 7), ("Z", 6, 3), ("Z", 5, 3), ("Y", 1, 0, 1, 2),
    ("XF", -1, 0, 2), ("SIB", 1, 1), ("ZW", 7), ("X", 1, 7, 1), ("XF", -1, 0, 3), ("ZT", 1, 2, 0), ("XF", 1, 0, 1), ("ZP", 5),
    ("SIB", 1, -1), ("Y", 1, 0, 1, 6), ("SIB", 4, -1), ("SIB", 7, 0), ("SIB", 1, 2), ("Y", 1, 0, 1, 7), ("ZT", 2, 2, 0),
    ("SIB", 4, 0), ("Y", -1, 0, 1, 5), ("YF", 1, 0, 1, 2), ("X", -1, 7, 1), ("X", 1, 6, 2), ("SIB", 0, 0), ("Y", 1, 0, 1, 5),
    ("Y", -1, 0, 1, 6), ("X", -1, 7, 3), ("X", 1, 7, 3), ("SIB", 4, 1), ("X", 1, 6, 3), ("ZP", 2), ("X", 1, 7, 2),
    ("SIB", 4, 2), ("Y", -1, 0, 1, 2), ("YF", 1, 0, 1, 6), ("ZW", 6), ("X", -1, 6, 1), ("ZT", -1, 2, 1), ("X", 1, 6, 1),
    ("X", 1, 3, 1), ("SQ", 1, 0), ("YF", -1, 0, 1, 5), ("XF", -1, 7, 2), ("SIB", 3, 0), ("X", -1, 6, 3), ("SIB", 0, 1),
    ("ZT", 1, 2, 1), ("XF", -1, 6, 2), ("SIB", 0, -1), ("XF", 1, 7, 1), ("SQ", 4, 0), ("SIB", 0, 2), ("SQ", 1, 1),
    ("SQ", 4, 1), ("SQ", 4, 2), ("SQ", 1, 2), ("XF", -1, 7, 3), ("ES", 1), ("Y", 1, 1, 0, 4), ("XF", 1, 6, 0), ("SQ", 0, 0),
    ("X", -1, 6, 0), ("SQ", 0, 1), ("SQ", 0, 2), ("SIB", 6, 0), ("ES", 4), ("ZT", 2, 2, 1), ("SIB", 7, -1), ("XF", 1, 6, 1),
    ("X", 1, 5, 0), ("XF", -1, 6, 3), ("ZW", 2), ("Y", -1, 1, 0, 4), ("Y", 1, 1, 0, 1), ("Y", 1, 1, 0, 0), ("X", -1, 3, 3),
    ("X", -1, 3, 2), ("X", -1, 3, 1), ("SIB", 7, 1), ("YF", 1, 1, 0, 4), ("SIB", 6, -1), ("ZT", -1, 2, 2), ("X", -1, 5, 3),
    ("Y", -1, 1, 0, 0), ("X", 1, 3, 2), ("ZT", 1, 2, 2), ("SIB", 7, 2), ("SX", 7, -1), ("Y", -1, 1, 0, 1), ("SX", 7, 0),
    ("Y", 1, 1, 1, 1), ("X", 1, 3, 3), ("SX", 7, 1), ("X", -1, 5, 2), ("SIB", 6, 1), ("SIB", 6, 2), ("SIB", 2, 0), ("ZW", 5),
    ("YF", 1, 1, 0, 0), ("SX", 7, 2), ("Y", -1, 1, 1, 1), ("XF", 1, 3, 1), ("Y", -1, 1, 1, 4), ("X", 1, 5, 3),
    ("ZT", 2, 2, 2), ("Y", -1, 1, 0, 7), ("ES", 7), ("Y", 1, 1, 0, 8), ("ZT", -1, 2, 3), ("Y", 1, 1, 1, 4), ("ES", 0),
    ("Y", 1, 1, 0, 7), ("X", 1, 5, 1), ("SIB", 2, -1), ("ZT", 1, 2, 3), ("XF", -1, 3, 3), ("YF", -1, 1, 0, 1), ("SIB", 2, 1),
    ("XF", 1, 3, 0), ("SQ", 6, 0), ("ZT", 2, 2, 3), ("SIB", 2, 2), ("SQ", 6, 1), ("SQ", 6, 2), ("Y", 1, 1, 0, 6),
    ("XF", -1, 3, 2), ("YF", -1, 1, 1, 1), ("SIB", 3, 1), ("X", 1, 5, 2), ("X", -1, 5, 1), ("ES", 8), ("XF", 1, 5, 0),
    ("XF", -1, 5, 3), ("ES", 6), ("YF", 1, 1, 0, 8), ("SIB", 3, -1), ("SQ", 2, 0), ("Y", -1, 1, 0, 6), ("YF", 1, 1, 1, 4),
    ("SQ", 2, 1), ("SQ", 2, 2), ("XF", -1, 5, 2), ("ES", 2), ("Y", -1, 1, 1, 7), ("Y", 1, 1, 0, 2), ("Y", -1, 1, 0, 2),
    ("XF", 1, 5, 1), ("SIB", 3, 2), ("Y", 1, 1, 1, 0), ("Y", 1, 1, 1, 8), ("YF", -1, 1, 0, 7), ("Y", 1, 1, 1, 7),
    ("SIB", 5, -1), ("SIB", 5, 1), ("Y", -1, 1, 1, 8), ("SIB", 5, 0), ("SQ", 3, 0), ("Y", -1, 1, 1, 0), ("YF", 1, 1, 0, 6),
    ("YF", -1, 1, 1, 7), ("SIB", 5, 2), ("SQ", 3, 1), ("SQ", 3, 2), ("Y", -1, 1, 1, 6), ("Y", -1, 1, 0, 3), ("Y", 1, 1, 1, 6),
    ("Y", 1, 1, 0, 3), ("YF", 1, 1, 1, 8), ("ES", 3), ("YF", 1, 1, 1, 0), ("SQ", 5, 0), ("SQ", 5, 1), ("SQ", 5, 2), ("ES", 5),
    ("Y", -1, 1, 0, 5), ("Y", -1, 1, 0, 8), ("CU", 1, 0), ("CU", 2, 0), ("Y", 1, 1, 0, 5), ("Y", -1, 1, 1, 2),
    ("YF", 1, 1, 1, 6), ("CU", 1, 3), ("Y", 1, 1, 1, 2), ("CU", 2, 3), ("YF", -1, 1, 0, 5), ("Y", 1, 1, 1, 3),
    ("Y", -1, 1, 1, 3), ("YF", 1, 1, 0, 2), ("CU", 3, 0), ("CU", 0, 0), ("CU", 0, 2), ("Y", -1, 1, 1, 5), ("YF", -1, 1, 0, 3),
    ("Y", 1, 1, 1, 5), ("CU", 3, 3), ("CU", 1, 2), ("YF", 1, 1, 1, 2), ("CU", 0, 3), ("YF", -1, 1, 1, 3), ("CU", 2, 1),
    ("YF", -1, 1, 1, 5), ("CU", 0, 1), ("CU", 1, 1), ("CU", 2, 2), ("CU", 3, 1), ("CU", 3, 2),
)


def mod4(v):
    return lax.rem(v + 8, 4)


class Step:
    def __init__(self, refs):
        (self.order_in, self.occupancy_in, self.square_in, self.cube_in, self.p_in, self.out, self.order, self.occupancy,
         self.square_pattern, self.cube_pattern, self.panel, self.p_cols, self.s_cols, self.square, self.cube, self.in_sem,
         self.send_sem, self.z_recv, self.x_recv, self.far_recv, self.exchange_recv, self.pass_recv, self.y_recv,
         self.sib_recv) = refs
        self.y, self.zh, self.zl, self.x, self.core = (lax.axis_index(name) for name in AXES)
        self.step = self.panel.shape[2] // CHUNKS
        self.waited = set()
        pair = lax.rem(self.zl, 2)
        half = self.zl // 2
        self.places = (self.zl, self.zl + 1 - 2 * pair, 2 - half, 3 - 3 * half)

    def at_x(self, d):
        return {"x": mod4(self.x + d)}

    def at_y(self, d):
        return {"y": mod4(self.y + d)}

    def at_z(self, d):
        z = lax.rem(self.zh * 4 + self.zl + d + 8, 8)
        return {"zh": z // 4, "zl": lax.rem(z, 4)}

    def other_core(self):
        return {"core": 1 - self.core}

    def rows(self, j):
        return pl.ds(j * self.step, self.step)

    def square_rows(self, j):
        if j not in (LAST, CHUNKS):
            return self.rows(j)
        return pl.ds(LAST * self.step + (self.step // 2 if j == CHUNKS else 0), self.step // 2)

    def half_rows(self, j, sign):
        return pl.ds(j * self.step + (0 if sign > 0 else self.step // 2), self.step // 2)

    def panel_at(self, g, zl, j):
        return self.panel.at[self.core, mod4(self.x + g) * 4 + zl, self.rows(j)]

    def half_at(self, g, j, sign):
        return self.panel.at[self.core, mod4(self.x + g) * 4 + self.zl, self.half_rows(j, sign)]

    def group(self, h, d):
        return 2 * mod4(self.y + d) + (self.zh if h == 0 else 1 - self.zh)

    def cols_at(self, phase, h, d, j):
        if phase == 0:
            return self.p_cols.at[self.group(h, d), self.rows(j)]
        return self.s_cols.at[self.group(h, d), self.square_rows(j)]

    def send(self, src, dst, kind, recv_sem, device, guard=None):
        copy = pltpu.make_async_remote_copy(
            src_ref=src, dst_ref=dst, send_sem=self.send_sem.at[kind], recv_sem=recv_sem, device_id=device,
            device_id_type=pl.DeviceIdType.MESH)
        if guard is None:
            copy.start()
        else:
            pl.when(guard)(copy.start)

    def arrived(self, key, dst, recv_sem, guard=None):
        if key in self.waited:
            return
        self.waited.add(key)
        copy = pltpu.make_async_remote_copy(
            src_ref=dst, dst_ref=dst, send_sem=recv_sem, recv_sem=recv_sem, device_id=self.other_core(),
            device_id_type=pl.DeviceIdType.MESH)
        if guard is None:
            copy.wait_recv()
        else:
            pl.when(guard)(copy.wait_recv)

    def sends_done(self, kind, tiles, rows, guard=None):
        part = self.panel.at[0, pl.ds(0, tiles), pl.ds(0, rows)]
        copy = pltpu.make_async_remote_copy(
            src_ref=part, dst_ref=part, send_sem=self.send_sem.at[kind], recv_sem=self.send_sem.at[kind],
            device_id=self.other_core(), device_id_type=pl.DeviceIdType.MESH)
        if guard is None:
            copy.wait_send()
        else:
            pl.when(guard)(copy.wait_send)

    def all_sends_done(self):
        step, first = self.step, len(X_FIRST)
        plain = CHUNKS - first
        end = (self.zl == 0) | (self.zl == 3)
        middle = (self.zl == 1) | (self.zl == 2)
        self.sends_done(0, plain, 8 * step)
        self.sends_done(1, plain, 4 * step)
        self.sends_done(2, 3, CHUNKS * step, end)
        self.sends_done(2, 5, CHUNKS * step, middle)
        self.sends_done(3, 6, CHUNKS * step)
        self.sends_done(4, 6, CHUNKS * step)
        self.sends_done(5, 1, CHUNKS * step)
        self.sends_done(6, 16, CHUNKS * step)
        if first:
            self.sends_done(7, 3 * first, step)
            self.sends_done(8, 3 * first, step, end)
            self.sends_done(8, 15 * first, step, middle)

    def x_arrived(self, g, j, o):
        self.arrived(("x", g, j, o), self.panel_at(g, self.places[o], j), self.x_sem(g, j, o))

    def x_sem(self, g, j, o):
        alone = o < 2 if g == -1 else o >= 2
        return self.x_recv.at[(g + 1) // 2, j, o % 2 if alone or j in X_FIRST else 2]

    def half_arrived(self, j, sign):
        self.arrived(("h", j, sign), self.half_at(2, j, sign), self.far_recv.at[j, (1 - sign) // 2])

    def group_arrived(self, g, j):
        if j not in X_FIRST and g == 2:
            tiles = self.panel.at[self.core, pl.ds(mod4(self.x + 2) * 4, 4), self.rows(j)]
            self.arrived(("g", j), tiles, self.far_recv.at[j, 0])
        elif j not in X_FIRST:
            for o in ((0, 1) if g == -1 else (2, 3)):
                self.x_arrived(g, j, o)
            pair = self.panel.at[self.core, pl.ds(0, 2), self.rows(j)]
            self.arrived(("p", g, j), pair, self.x_recv.at[(g + 1) // 2, j, 2])
        elif g == 2:
            self.half_arrived(j, 1)
            self.half_arrived(j, -1)
        else:
            self.x_arrived(g, j, 0)

    def passed_on(self, d, j):
        return d == (-1 if j % 2 == 0 else 1)

    def span(self, j):
        return (LAST if j == CHUNKS else j) // SPAN

    def y_sem(self, phase, h, d, j):
        if d == 0:
            return self.exchange_recv.at[phase, j]
        if self.passed_on(d, j):
            return self.pass_recv.at[phase, h, j]
        return self.y_recv.at[h, int(d == 2), 0 if phase == 0 else 1 + self.span(j)]

    def y_arrived(self, phase, h, d, j):
        if d == 0 or self.passed_on(d, j):
            self.arrived(("y", phase, h, d, j), self.cols_at(phase, h, d, j), self.y_sem(phase, h, d, j))
        elif phase == 0:
            self.arrived(("late", 0, h, d == 2), self.p_cols.at[self.group(h, d)], self.y_sem(0, h, d, j))
        else:
            span = self.span(j)
            part = self.s_cols.at[self.group(h, d), pl.ds(span * 256, 256)]
            self.arrived(("late", 1, h, d == 2, span), part, self.y_sem(1, h, d, j))

    def line(self, g, j, d, kind, at):
        zl = self.zl
        low = self.panel_at(g, lax.max(zl - d, 0), j)
        high = self.panel_at(g, lax.min(zl + d, 3), j)
        end = (zl == 0) | (zl == 3)
        if d == 1:
            both = self.panel.at[self.core, pl.ds(0, 2), self.rows(j)]
            self.arrived(("z", g, j, 1, 2), both, self.z_recv.at[at, 0], (zl == 1) | (zl == 2))
        if d == 3 or d == 1 and g != 0:
            self.arrived(("z", g, j, d), low, self.z_recv.at[at, d - 1], end)
        elif d == 2:
            self.arrived(("z", g, j, 2), low, self.z_recv.at[at, 1])
        if d < 3:
            self.send(low, low, kind, self.z_recv.at[at, d], self.at_z(1), (zl >= d) & (zl < 3))
            self.send(high, high, kind, self.z_recv.at[at, d], self.at_z(-1), (zl <= 3 - d) & (zl > 0))

    def Z(self, j, d):
        if d == 0:
            tile = self.panel_at(0, self.zl, j)
            self.send(tile, tile, 2, self.z_recv.at[j, 0], self.at_z(1), self.zl < 2)
            self.send(tile, tile, 2, self.z_recv.at[j, 0], self.at_z(-1), self.zl >= 2)
            return
        self.line(0, j, d, 2, j)
        if d >= 2:
            far = 4 - d
            mine = self.p_cols.at[self.group(0, 0), self.rows(j)]
            self.send(self.panel_at(0, 3 - d, j), mine, 2, self.y_sem(0, 1, 0, j), self.at_z(far), self.zl == 3)
            self.send(self.panel_at(0, d, j), mine, 2, self.y_sem(0, 1, 0, j), self.at_z(-far), self.zl == 0)

    def ZW(self, j):
        end = (self.zl == 0) | (self.zl == 3)
        self.arrived(("z", 0, j, 1), self.panel_at(0, self.places[1], j), self.z_recv.at[j, 0], end)

    def ZP(self, j):
        tile = self.panel_at(0, self.zl, j)
        self.send(tile, tile, 2, self.z_recv.at[j, 0], self.at_z(-1), self.zl == 1)
        self.send(tile, tile, 2, self.z_recv.at[j, 0], self.at_z(1), self.zl == 2)

    def ZT(self, g, j, d):
        if d == 0:
            self.group_arrived(g, j)
        self.line(g, j, d, 8, CHUNKS + 3 * X_FIRST.index(j) + g % 4 - 1)

    def X(self, sign, j, o):
        tile = self.panel_at(0, self.places[o], j)
        self.send(tile, tile, 7 if j in X_FIRST else 0, self.x_sem(-sign, j, o), self.at_x(sign))

    def XF(self, sign, j, o):
        self.x_arrived(-sign, j, o)
        tile = self.panel_at(-sign, self.places[o], j)
        self.send(tile, tile, 1, self.far_recv.at[j, 0], self.at_x(sign))

    def XH(self, sign, j):
        self.x_arrived(-sign, j, 0)
        tile = self.half_at(-sign, j, sign)
        self.send(tile, tile, 7, self.far_recv.at[j, (1 - sign) // 2], self.at_x(sign))

    def Y(self, sign, phase, h, j):
        if h == 1:
            self.y_arrived(phase, 1, 0, j)
        tile = self.cols_at(phase, h, 0, j)
        self.send(tile, tile, 3 + phase, self.y_sem(phase, h, -sign, j), self.at_y(sign))

    def YF(self, sign, phase, h, j):
        self.y_arrived(phase, h, -sign, j)
        tile = self.cols_at(phase, h, -sign, j)
        self.send(tile, tile, 3 + phase, self.y_sem(phase, h, 2, j), self.at_y(sign))

    def ES(self, j):
        tile = self.cols_at(1, 0, 0, j)
        self.send(tile, tile, 5, self.y_sem(1, 1, 0, j), self.at_z(4))

    def SIB(self, j, g):
        if g != 0:
            self.group_arrived(g, j)
        tiles = self.panel.at[self.core, pl.ds(mod4(self.x + g) * 4, 4), self.rows(j)]
        self.send(tiles, tiles, 6, self.sib_recv.at[CHUNKS + g % 4 if j == LAST else j],
                  self.other_core())

    def sibling_arrived(self, j):
        self.arrived(("s", j), self.panel.at[1 - self.core, :, self.rows(j)], self.sib_recv.at[j])

    def sibling_group_arrived(self, j, g):
        tiles = self.panel.at[1 - self.core, pl.ds(mod4(self.x + g) * 4, 4), self.rows(j)]
        self.arrived(("sg", j, g), tiles, self.sib_recv.at[CHUNKS + g % 4])

    def square_terms(self, j, y, zh):
        total = None
        for t in range(4):
            left = self.panel[t % 2, (2 * zh + t // 2) * 4 + y, self.rows(j), :]
            right = self.p_cols[2 * y + zh, pl.ds(t * 256, 256), :]
            term = jnp.dot(left, right, preferred_element_type=jnp.float32)
            total = term if total is None else total + term
        return total

    def SQ(self, j, part):
        h = min(part, 1)
        for d in ((-1, 1, 2), (0, -1, 1), (2,))[part]:
            for i in range(CHUNKS):
                self.y_arrived(0, h, d, i)
        if part == 0:
            self.sibling_arrived(j)
        zh = self.zh if h == 0 else 1 - self.zh
        first, count = ((0, 4), (self.y - 1, 3), (self.y + 2, 1))[part]

        def add(i, carry):
            self.square[self.rows(j), :] += self.square_terms(j, mod4(first + i), zh)
            return carry

        lax.fori_loop(0, count, add, 0)
        if part == 2:
            self.keep_square(j)

    def SX(self, j, g):
        for h in (0, 1):
            for d in (0, -1, 1, 2):
                for i in range(CHUNKS):
                    if (h, d) != (0, 0):
                        self.y_arrived(0, h, d, i)
        if g != 0:
            self.group_arrived(g, j)
        self.sibling_group_arrived(j, g)
        x = mod4(self.x + g)
        zh, pair = x // 2, lax.rem(x, 2)

        def add(zl, carry):
            total = None
            for core in range(2):
                left = self.panel[core, x * 4 + zl, self.rows(j), :]
                right = self.p_cols[2 * zl + zh, pl.ds(pl.multiple_of((2 * pair + core) * 256, 256), 256), :]
                term = jnp.dot(left, right, preferred_element_type=jnp.float32)
                total = term if total is None else total + term
            self.square[self.rows(j), :] += total
            return carry

        lax.fori_loop(0, 4, add, 0)
        if g == 2:
            self.keep_square(j)

    def keep_square(self, j):
        mine = self.group(0, 0)
        for i, q, keep in self.flags(self.square_pattern, j):
            at = (pl.ds(i * 128, 128), pl.ds(q * 128, 128))
            block = self.square[at] * keep
            self.square[at] = block
            self.s_cols[(mine,) + at] = block.astype(jnp.bfloat16)

    def CU(self, sources, j, last=False):
        terms = []
        parts = list(range(j * SPAN, (j + 1) * SPAN)) + ([CHUNKS] if LAST // SPAN == j else [])
        for h, d in SOURCES[sources]:
            for i in parts:
                if (h, d) != (0, 0):
                    self.y_arrived(1, h, d, i)
            terms.append((mod4(self.y + d), self.zh if h == 0 else 1 - self.zh))

        def add(i, carry):
            rows = pl.ds(pl.multiple_of(i * 512, 512), 512)
            total = None
            for y, zh in terms:
                left = self.panel[j % 2, (2 * zh + j // 2) * 4 + y, rows, :]
                right = self.s_cols[2 * y + zh, pl.ds(j * 256, 256), :]
                term = jnp.dot(left, right, preferred_element_type=jnp.float32)
                total = term if total is None else total + term
            if last:
                total += self.cube[rows, :]
                for r in range(4):
                    for q in range(2):
                        at = (pl.ds(pl.multiple_of(i * 512 + r * 128, 128), 128), pl.ds(q * 128, 128))
                        block = total[r * 128:(r + 1) * 128, q * 128:(q + 1) * 128]
                        self.out[at] = 3.0 * self.square[at] - 2.0 * (block * self.flag(self.cube_pattern, 4 * i + r, q))
            else:
                self.cube[rows, :] += total
            return carry

        lax.fori_loop(0, 2, add, 0)

    def flag(self, pattern, i, q):
        a = self.order[self.group(0, 0) * 8 + i]
        b = self.order[((self.zl * 4 + self.x) * 2 + self.core) * 2 + q]
        kept = pattern[lax.min(a, b), lax.max(a, b)]
        return jnp.where(kept > 0, jnp.float32(1), jnp.float32(0))

    def flags(self, pattern, j):
        count = self.step // 128
        for i in range(j * count, (j + 1) * count):
            for q in range(2):
                yield i, q, self.flag(pattern, i, q)

    def run(self):
        mine, place = self.group(0, 0), self.x * 4 + self.zl
        inputs = [
            pltpu.make_async_copy(src, dst, self.in_sem.at[i]) for i, (src, dst) in enumerate((
                (self.order_in, self.order), (self.occupancy_in, self.occupancy),
                (self.p_in, self.panel.at[self.core, place]),
                (self.square_in, self.square_pattern), (self.cube_in, self.cube_pattern)))]
        for copy in inputs:
            copy.start()
        barrier = pltpu.get_barrier_semaphore()
        partners = [self.at_x(1), self.at_x(-1), self.at_y(1), self.at_y(-1), self.at_z(1), self.at_z(-1), self.at_z(2),
                    self.at_z(-2), self.other_core()]
        for device in partners:
            pl.semaphore_signal(barrier, inc=1, device_id=device, device_id_type=pl.DeviceIdType.MESH)
        for copy in inputs:
            copy.wait()
        for j in range(CHUNKS):
            for i, q, keep in self.flags(self.occupancy, j):
                at = (pl.ds(i * 128, 128), pl.ds(q * 128, 128))
                block = (self.panel[(self.core, place) + at].astype(jnp.float32) * keep).astype(jnp.bfloat16)
                self.panel[(self.core, place) + at] = block
                self.p_cols[(mine,) + at] = block
        self.square[...] = jnp.zeros_like(self.square)
        self.cube[...] = jnp.zeros_like(self.cube)
        pl.semaphore_wait(barrier, len(partners))
        for name, *args in ORDER[:-1]:
            getattr(self, name)(*args)
        self.CU(*ORDER[-1][1:], last=True)
        self.all_sends_done()


def kernel(*refs):
    Step(refs).run()


def body(p_values, occupancy, square_pattern, cube_pattern, block_order):
    rows, cols = p_values.shape
    hbm = pl.BlockSpec(memory_space=pltpu.HBM)
    sem = pltpu.SemaphoreType.DMA
    lines = CHUNKS + 3 * len(X_FIRST)
    return pl.pallas_call(
        kernel,
        out_shape=jax.ShapeDtypeStruct((rows, cols), jnp.float32),
        in_specs=[hbm] * 5,
        out_specs=pl.BlockSpec(memory_space=pltpu.VMEM),
        scratch_shapes=[
            pltpu.SMEM(block_order.shape, jnp.int32),
            pltpu.SMEM(occupancy.shape, jnp.int32),
            pltpu.SMEM(occupancy.shape, jnp.int32),
            pltpu.SMEM(occupancy.shape, jnp.int32),
            pltpu.VMEM((2, 16, rows, cols), jnp.bfloat16),
            pltpu.VMEM((8, rows, cols), jnp.bfloat16),
            pltpu.VMEM((8, rows, cols), jnp.bfloat16),
            pltpu.VMEM((rows, cols), jnp.float32),
            pltpu.VMEM((rows, cols), jnp.float32),
            sem((5,)),
            sem((9,)),
            sem((lines, 3)),
            sem((2, CHUNKS, 3)),
            sem((CHUNKS, 2)),
            sem((2, CHUNKS + 1)),
            sem((2, 2, CHUNKS + 1)),
            sem((2, 2, 5)),
            sem((CHUNKS + 4,)),
        ],
        compiler_params=pltpu.CompilerParams(collective_id=0, has_side_effects=True, vmem_limit_bytes=48 * 2**20),
        cost_estimate=pl.CostEstimate(flops=4 * rows * cols * 8192, bytes_accessed=2**24, transcendentals=0),
    )(block_order, occupancy, square_pattern, cube_pattern, p_values)


def solution(mesh):
    finer = Mesh(mesh.devices.reshape(4, 2, 4, 4, 2), AXES)
    tiles = P(("y", "zh"), ("zl", "x", "core"))
    return jax.shard_map(
        body, mesh=finer, in_specs=(tiles, P(), P(), P(), P()), out_specs=tiles, check_vma=False
    )
```
